256 devices in a mesh: ctx: 64 (over x_hi, y, z), tp: 4 (over x_lo, core).
Axes of the slice: x: 4 (x_hi: 2, x_lo: 2; x = x_hi * 2 + x_lo), y: 4, z: 8, core: 2. Of those that a mesh axis runs over, the one named last changes fastest.
Arguments:
- hidden: bfloat16 [32768, 5120], P('ctx', 'tp'), may hold values from -6 to 6
- queries: bfloat16 [32768, 5120], P('ctx', 'tp'), may hold values from -600 to 600
- lengths: int32 [256], replicated, may hold values from 1 to 2048, 32768 in all
- norm_gain: float32 [5120], P('tp'), may hold values from 0.5 to 1.5
- kv_weight: bfloat16 [5120, 2, 1024], P(None, None, 'tp'), may hold values from -0.078125 to 0.078125
- kv_bias: float32 [2, 1024], P(None, 'tp'), may hold values from -3 to 3
Outputs:
- attended: bfloat16 [32768, 5120], P('ctx', 'tp')
The draws below stay inside these ranges and needn't reach their ends.
Inputs may be any that keep to these rules, and one draw needn't show every extreme that they name: The 256 files fill the 32768 positions in order; their lengths sum to 32768 and the longest is exactly 2048.
All inputs are finite; a program needn't handle non-finite values.
Results may differ from the reference program's by a relative error of at most 0.006.
Values may be sent and summed in bfloat16 or wider, within the bound.
A program may use at most 128 MiB of HBM per device.

```python
import math
import jax
import jax.numpy as jnp
import numpy as np
from jax import lax

D = 5120
QH = 40
KVH = 8
HD = 128
TOK_DEV = 512
TOKENS = 32768
NDOCS = 256
FILE_MAX = 2048
N_CTX = 64


def draw_queries(key, part):
    key_base = jax.random.fold_in(key, 0)
    shape = (TOKENS, QH * HD)
    return jnp.clip(jax.random.normal(key_base, shape, jnp.float32), -6.0, 6.0).astype(jnp.bfloat16)


def block_levels(rng, shape, shards, smallest, top_value):
    level, own = 1.0, jax.random.fold_in(rng, 6)
    for axis_at, shards_of in shards:
        heights = jnp.exp(jax.random.uniform(jax.random.fold_in(own, axis_at), (shards_of,), jnp.float32, smallest / len(shards), top_value / len(shards)))
        level = level * jnp.repeat(heights, shape[axis_at] // shards_of).reshape([-1 if axis == axis_at else 1 for axis in range(len(shape))])
    return level


def length_profile(number_of, total, limit, skew):
    loads = [(1 << 20) // math.isqrt(grade ** skew) + 1 for grade in range(2, number_of + 1)]
    spare, counts = total - limit - (number_of - 1), [1] * (number_of - 1)
    while spare > 0:
        free = [i for i in range(number_of - 1) if counts[i] < limit]
        pool, remaining = sum([loads[i] for i in free]), spare
        for i in free:
            more = min(limit - counts[i], max(1, remaining * loads[i] // pool), spare)
            counts[i] = counts[i] + more
            spare = spare - more
    return np.array([limit] + counts)


def uneven(rng, amount, total, bound, lean):
    if amount == 2:
        one = jax.random.randint(rng, (), max(1, total - bound), min(bound, total - 1) + 1)
        return jnp.stack([one, total - one])
    sizes = jnp.asarray(length_profile(amount, total, bound, lean), jnp.int32)
    twos = (amount - 1) // 2
    donor, sink = sizes[1:1 + 2 * twos:2], sizes[2:2 + 2 * twos:2]
    margin = jnp.minimum(donor - 1, bound - sink)
    shifted = jax.random.randint(jax.random.fold_in(rng, 1), (twos,), 0, 1 << 20) % (margin + 1)
    sizes = sizes.at[1:1 + 2 * twos:2].set(donor - shifted).at[2:2 + 2 * twos:2].set(sink + shifted)
    return sizes[jax.random.permutation(jax.random.fold_in(rng, 2), amount)]


def gaussian(own_key, extent, spread, most, cuts=(), kind=jnp.bfloat16):
    loudness = block_levels(own_key, extent, cuts, -0.22, 0.18) if cuts else 1.0
    values = jax.random.normal(own_key, extent, jnp.float32) * spread * loudness
    return jnp.minimum(jnp.maximum(values, -most), most).astype(kind)


def setup_inputs(seed: int = 0) -> dict:
    key_list = jax.random.split(jax.random.key(seed), 7)
    return {
        "hidden": gaussian(key_list[0], (TOKENS, D), 1.0, 6.0, ((0, 64), (1, 4))),
        "queries": draw_queries(jax.random.fold_in(key_list[6], 71), 0),
        "lengths": uneven(key_list[2], NDOCS, TOKENS, FILE_MAX, 2).astype(jnp.int32),
        "norm_gain": jnp.clip(1.0 + 0.1 * jax.random.normal(key_list[3], (D,), jnp.float32), 0.5, 1.5),
        "kv_weight": gaussian(key_list[4], (D, 2, KVH * HD), D ** -0.5, 0.078125, ((2, 4),)),
        "kv_bias": gaussian(key_list[5], (2, KVH * HD), 0.5, 3.0, ((1, 4),), jnp.float32),
    }


def doc_ids(positions, lengths):
    ends = jnp.cumsum(lengths).astype(jnp.int32)
    return lax.optimization_barrier(jnp.sum((positions[:, None] >= ends[None, :]).astype(jnp.int32), axis=1)).astype(jnp.int32)

def reference(hidden, queries, lengths, norm_gain, kv_weight, kv_bias):
    xfull = hidden.astype(jnp.float32)
    scale_rows = lax.rsqrt(lax.optimization_barrier(jnp.mean(xfull * xfull, axis=1, keepdims=True)) + 1e-06)
    normed = (xfull * scale_rows * norm_gain.astype(jnp.float32)[None, :]).astype(jnp.bfloat16)
    flat = jnp.dot(normed, kv_weight.reshape(D, 2 * KVH * HD), preferred_element_type=jnp.float32)
    flat = flat + kv_bias.astype(jnp.float32).reshape(-1)[None, :]
    kv_all = flat.astype(jnp.bfloat16).reshape(TOKENS, 2, KVH, HD)
    kv_pad = jnp.concatenate([jnp.zeros((FILE_MAX, 2, KVH, HD), kv_all.dtype), kv_all], axis=0)
    positions = jnp.arange(TOKENS, dtype=jnp.int32)
    docs = doc_ids(positions, lengths)
    docs_pad = jnp.concatenate([jnp.full((FILE_MAX,), -1, jnp.int32), docs])
    pos_pad = jnp.concatenate([jnp.arange(FILE_MAX, dtype=jnp.int32) - FILE_MAX, positions])
    group = QH // KVH
    score_scale = HD ** (-0.5)

    def one_block(block):
        first = (block * TOK_DEV).astype(jnp.int32)
        qrows = lax.dynamic_slice_in_dim(queries, first, TOK_DEV, 0).astype(jnp.float32)
        qrows = qrows.reshape(TOK_DEV, KVH, group, HD)
        window = lax.dynamic_slice_in_dim(kv_pad, first, FILE_MAX + TOK_DEV, 0).astype(jnp.float32)
        kdoc = lax.dynamic_slice_in_dim(docs_pad, first, FILE_MAX + TOK_DEV, 0)
        kpos = lax.dynamic_slice_in_dim(pos_pad, first, FILE_MAX + TOK_DEV, 0)
        qdoc = lax.dynamic_slice_in_dim(docs, first, TOK_DEV, 0)
        qpos = lax.dynamic_slice_in_dim(positions, first, TOK_DEV, 0)
        scores = jnp.einsum('qgjd,kgd->gjqk', qrows, window[:, 0]) * score_scale
        visible = (qdoc[:, None] == kdoc[None, :]) & (kpos[None, :] <= qpos[:, None])
        scores = jnp.where(visible[None, None], scores, -1e+30)
        top = lax.optimization_barrier(jnp.max(scores, axis=-1, keepdims=True))
        probs = jnp.exp(scores - top)
        total = lax.optimization_barrier(jnp.sum(probs, axis=-1))
        rounded = lax.optimization_barrier(probs.astype(jnp.bfloat16)).astype(jnp.float32)
        summed = jnp.einsum('gjqk,kgd->gjqd', rounded, window[:, 1])
        result = summed / total[..., None]
        return result.transpose(2, 0, 1, 3).reshape(TOK_DEV, QH * HD).astype(jnp.bfloat16)
    blocks = lax.map(one_block, jnp.arange(N_CTX, dtype=jnp.int32))
    return blocks.reshape(TOKENS, QH * HD)
```

```python
import jax
import jax.numpy as jnp
from jax import lax
from jax.sharding import PartitionSpec as P

D = 5120
HD = 128
CYCLE = 4


def shifted(value, axis, steps):
    count = lax.axis_size(axis)
    leading, last = (max(0, -steps), min(count, count - steps))
    return lax.ppermute(value, axis, [(source, source + steps) for source in range(leading, last)])


def flipped(value, axis, bit):
    count = lax.axis_size(axis)
    return lax.ppermute(value, axis, [(source, source ^ bit) for source in range(count)])


def body(hidden, queries, lengths, norm_gain, kv_weight, kv_bias):
    tok, width = hidden.shape
    tpi = lax.axis_index("tp")
    across = flipped(hidden, "tp", 2)
    pair = flipped(jnp.stack([hidden, across]), "tp", 1)
    blocks = [(hidden, tpi), (across, tpi ^ 2), (pair[0], tpi ^ 1), (pair[1], tpi ^ 3)]
    gain_all = lax.all_gather(norm_gain, "tp", tiled=True)
    squares = None
    for part, _ in blocks:
        xf = part.astype(jnp.float32)
        term = jnp.sum(xf * xf, axis=1)
        squares = term if squares is None else squares + term
    scale_rows = lax.rsqrt(squares / D + 1e-06)
    flat_weight = kv_weight.reshape(kv_weight.shape[0], -1)
    summed = None
    for part, owner in blocks:
        gain = lax.dynamic_slice_in_dim(gain_all, owner * width, width)
        normed = (part.astype(jnp.float32) * scale_rows[:, None] * gain[None, :]).astype(jnp.bfloat16)
        rows = lax.dynamic_slice_in_dim(flat_weight, owner * width, width, 0)
        term = jnp.dot(normed, rows, preferred_element_type=jnp.float32)
        summed = term if summed is None else summed + term
    kv_local = (
        (summed + kv_bias.reshape(-1)[None, :])
        .astype(jnp.bfloat16)
        .reshape(tok, 2, kv_weight.shape[2])
    )
    kv_heads = kv_weight.shape[2] // HD
    group = queries.shape[1] // HD // kv_heads
    qrows = queries.reshape(tok, kv_heads, group, HD)
    device = lax.axis_index("ctx")
    ends = jnp.cumsum(lengths)
    score_scale = HD ** (-0.5)

    def docs_of(first):
        positions = first + jnp.arange(tok, dtype=jnp.int32)
        found = jnp.sum((positions[:, None] >= ends[None, :]).astype(jnp.int32), axis=1)
        return (found, positions)

    qdoc, qpos = docs_of(device * tok)

    def attend(state, block, back):
        best, mass, acc = state
        kdoc, kpos = docs_of((device - back) * tok)
        kdoc = jnp.where(device - back >= 0, kdoc, -1)
        keys = block[:, 0].reshape(tok, kv_heads, HD)
        values = block[:, 1].reshape(tok, kv_heads, HD)
        scores = (
            jnp.einsum("qgjd,kgd->gjqk", qrows, keys, preferred_element_type=jnp.float32)
            * score_scale
        )
        visible = (qdoc[:, None] == kdoc[None, :]) & (kpos[None, :] <= qpos[:, None])
        scores = jnp.where(visible[None, None], scores, -1e30)
        top = jnp.maximum(best, jnp.max(scores, axis=-1))
        probs = jnp.exp(scores - top[..., None])
        shrink = jnp.exp(best - top)
        mass = mass * shrink + jnp.sum(probs, axis=-1)
        acc = acc * shrink[..., None] + jnp.einsum(
            "gjqk,kgd->gjqd", probs.astype(jnp.bfloat16), values, preferred_element_type=jnp.float32
        )
        return (top, mass, acc)

    state = (
        jnp.full((kv_heads, group, tok), -1e30, jnp.float32),
        jnp.zeros((kv_heads, group, tok), jnp.float32),
        jnp.zeros((kv_heads, group, tok, HD), jnp.float32),
    )
    state = attend(state, kv_local, 0)
    moving = kv_local
    for back in range(1, CYCLE + 1):
        moving = shifted(moving, "ctx", 1)
        state = attend(state, moving, back)
    best, mass, acc = state
    result = acc / mass[..., None]
    return result.transpose(2, 0, 1, 3).reshape(tok, queries.shape[1]).astype(jnp.bfloat16)


def solution(mesh):
    in_specs = (P("ctx", "tp"), P("ctx", "tp"), P(), P("tp"), P(None, None, "tp"), P(None, "tp"))
    out_specs = P("ctx", "tp")
    return jax.shard_map(body, mesh=mesh, in_specs=in_specs, out_specs=out_specs, check_vma=False)
```

```python
import functools

import jax
import jax.numpy as jnp
from jax import lax
from jax.experimental import pallas as pl
from jax.experimental.pallas import tpu as pltpu
from jax.sharding import PartitionSpec as P

D = 5120
HD = 128
CYCLE = 4


def shifted(value, axis, steps):
    count = lax.axis_size(axis)
    leading, last = (max(0, -steps), min(count, count - steps))
    return lax.ppermute(value, axis, [(source, source + steps) for source in range(leading, last)])


def flipped(value, axis, bit):
    count = lax.axis_size(axis)
    return lax.ppermute(value, axis, [(source, source ^ bit) for source in range(count)])


def attention_kernel(group, tok, scale, nblocks_ref, q_ref, k_ref, v_ref, qdoc_ref, kdoc_ref,
                     o_ref, m_ref, l_ref, acc_ref):
    b = pl.program_id(1)
    last = pl.num_programs(1) - 1

    @pl.when(b < nblocks_ref[0])
    def _():
        same = qdoc_ref[...] == kdoc_ref[...]
        rows = lax.broadcasted_iota(jnp.int32, (tok, tok), 0)
        cols = lax.broadcasted_iota(jnp.int32, (tok, tok), 1)
        visible = same & ((b > 0) | (cols <= rows))
        keys = k_ref[...]
        values = v_ref[...]
        for j in range(group):
            q = q_ref[:, j * HD:(j + 1) * HD]
            s = lax.dot_general(q, keys, (((1,), (1,)), ((), ())),
                                preferred_element_type=jnp.float32) * scale
            s = jnp.where(visible, s, -1e30)
            top = jnp.max(s, axis=1, keepdims=True)

            @pl.when(b == 0)
            def _():
                p = jnp.exp(s - top)
                m_ref[j] = jnp.broadcast_to(top, (tok, HD))
                l_ref[j] = jnp.broadcast_to(jnp.sum(p, axis=1, keepdims=True), (tok, HD))
                acc_ref[j] = jnp.dot(p.astype(jnp.bfloat16), values,
                                     preferred_element_type=jnp.float32)

            @pl.when(b > 0)
            def _():
                prev = m_ref[j]
                best = jnp.maximum(prev, top)
                shrink = jnp.exp(prev - best)
                p = jnp.exp(s - best[:, :1])
                m_ref[j] = best
                l_ref[j] = l_ref[j] * shrink + jnp.sum(p, axis=1, keepdims=True)
                acc_ref[j] = acc_ref[j] * shrink + jnp.dot(
                    p.astype(jnp.bfloat16), values, preferred_element_type=jnp.float32)

    @pl.when(b == last)
    def _():
        for j in range(group):
            o_ref[:, j * HD:(j + 1) * HD] = (acc_ref[j] / l_ref[j]).astype(o_ref.dtype)


def attend_all(queries, kv_stack, qdoc, kdoc, nblocks, kv_heads):
    tok, width = queries.shape
    group = width // HD // kv_heads
    nb = kv_stack.shape[0] // tok

    def kv_index(kind):
        return lambda g, b, n: (jnp.minimum(b, n[0] - 1), kind * kv_heads + g)

    grid_spec = pltpu.PrefetchScalarGridSpec(
        num_scalar_prefetch=1,
        grid=(kv_heads, nb),
        in_specs=[
            pl.BlockSpec((tok, group * HD), lambda g, b, n: (0, g)),
            pl.BlockSpec((tok, HD), kv_index(0)),
            pl.BlockSpec((tok, HD), kv_index(1)),
            pl.BlockSpec((tok, 1), lambda g, b, n: (0, 0)),
            pl.BlockSpec((1, tok), lambda g, b, n: (0, jnp.minimum(b, n[0] - 1))),
        ],
        out_specs=pl.BlockSpec((tok, group * HD), lambda g, b, n: (0, g)),
        scratch_shapes=[
            pltpu.VMEM((group, tok, HD), jnp.float32),
            pltpu.VMEM((group, tok, HD), jnp.float32),
            pltpu.VMEM((group, tok, HD), jnp.float32),
        ],
    )
    return pl.pallas_call(
        functools.partial(attention_kernel, group, tok, HD ** (-0.5)),
        grid_spec=grid_spec,
        out_shape=jax.ShapeDtypeStruct((tok, width), queries.dtype),
        compiler_params=pltpu.CompilerParams(dimension_semantics=("arbitrary", "arbitrary")),
    )(nblocks, queries, kv_stack, kv_stack, qdoc, kdoc)


def body(hidden, queries, lengths, norm_gain, kv_weight, kv_bias):
    tok, width = hidden.shape
    tpi = lax.axis_index("tp")
    across = flipped(hidden, "tp", 2)
    pair = flipped(jnp.stack([hidden, across]), "tp", 1)
    gain_across = flipped(norm_gain, "tp", 2)
    gain_pair = flipped(jnp.stack([norm_gain, gain_across]), "tp", 1)
    blocks = [
        (hidden, norm_gain, tpi),
        (across, gain_across, tpi ^ 2),
        (pair[0], gain_pair[0], tpi ^ 1),
        (pair[1], gain_pair[1], tpi ^ 3),
    ]
    squares = None
    for part, _, _ in blocks:
        xf = part.astype(jnp.float32)
        term = jnp.sum(xf * xf, axis=1)
        squares = term if squares is None else squares + term
    scale_rows = lax.rsqrt(squares / D + 1e-06)
    flat_weight = kv_weight.reshape(kv_weight.shape[0], -1)
    summed = None
    for part, gain, owner in blocks:
        normed = (part.astype(jnp.float32) * scale_rows[:, None] * gain[None, :]).astype(jnp.bfloat16)
        rows = lax.dynamic_slice_in_dim(flat_weight, owner * width, width, 0)
        term = jnp.dot(normed, rows, preferred_element_type=jnp.float32)
        summed = term if summed is None else summed + term
    kv_local = (summed + kv_bias.reshape(-1)[None, :]).astype(jnp.bfloat16)
    kv_heads = kv_weight.shape[2] // HD

    device = lax.axis_index("ctx")
    ends = jnp.cumsum(lengths)
    backs = jnp.arange(CYCLE + 1, dtype=jnp.int32)
    starts = (device - backs) * tok
    positions = starts[:, None] + jnp.arange(tok, dtype=jnp.int32)[None, :]
    found = jnp.sum((positions[:, :, None] >= ends[None, None, :]).astype(jnp.int32), axis=2)
    kdoc = jnp.where((device - backs >= 0)[:, None], found, -1)
    qdoc = found[0]
    reach = jnp.sum((kdoc[:, tok - 1] >= qdoc[0]).astype(jnp.int32))
    nblocks = jnp.reshape(reach, (1,))

    moving = kv_local
    stack = [kv_local]
    for back in range(1, CYCLE + 1):
        moving = shifted(moving, "ctx", 1)
        stack.append(moving)
    kv_stack = jnp.concatenate(stack, axis=0)
    return attend_all(queries, kv_stack, qdoc[:, None], kdoc.reshape(1, -1), nblocks, kv_heads)


def solution(mesh):
    in_specs = (P("ctx", "tp"), P("ctx", "tp"), P(), P("tp"), P(None, None, "tp"), P(None, "tp"))
    out_specs = P("ctx", "tp")
    return jax.shard_map(body, mesh=mesh, in_specs=in_specs, out_specs=out_specs, check_vma=False)
```

```python
import functools

import jax
import jax.numpy as jnp
from jax import lax
from jax.experimental import pallas as pl
from jax.experimental.pallas import tpu as pltpu
from jax.sharding import PartitionSpec as P

D = 5120
HD = 128
CYCLE = 4


def shifted(value, axis, steps):
    count = lax.axis_size(axis)
    leading, last = (max(0, -steps), min(count, count - steps))
    return lax.ppermute(value, axis, [(source, source + steps) for source in range(leading, last)])


def flipped(value, axis, bit):
    count = lax.axis_size(axis)
    return lax.ppermute(value, axis, [(source, source ^ bit) for source in range(count)])


def ring_kernel(group, tok, scale, q_ref, kv_ref, qdoc_ref, kdoc_ref, o_ref,
                recv, send_sem, recv_sem, m_ref, l_ref, acc_ref, bias_ref):
    c = lax.axis_index("ctx")
    t = lax.axis_index("tp")
    n = lax.axis_size("ctx")
    heads = q_ref.shape[1] // HD
    kv_width = kv_ref.shape[1] // 2
    half = tok // 2

    barrier = pltpu.get_barrier_semaphore()

    @pl.when(c > 0)
    def _():
        pl.semaphore_signal(barrier, inc=1, device_id=(c - 1, t), device_id_type=pl.DeviceIdType.MESH)

    @pl.when(c < n - 1)
    def _():
        pl.semaphore_signal(barrier, inc=1, device_id=(c + 1, t), device_id_type=pl.DeviceIdType.MESH)

    peers = (c > 0).astype(jnp.int32) + (c < n - 1).astype(jnp.int32)
    pl.semaphore_wait(barrier, peers)

    def copy_of(step):
        src = kv_ref if step == 0 else recv.at[step - 1]
        return pltpu.make_async_remote_copy(
            src_ref=src, dst_ref=recv.at[step], send_sem=send_sem.at[step],
            recv_sem=recv_sem.at[step], device_id=(c + 1, t),
            device_id_type=pl.DeviceIdType.MESH)

    def sends_at(step):
        return (c >= step) & (c < n - 1)

    m_ref[...] = jnp.full(m_ref.shape, -1e30, jnp.float32)
    l_ref[...] = jnp.zeros(l_ref.shape, jnp.float32)
    acc_ref[...] = jnp.zeros(acc_ref.shape, jnp.float32)

    def compute(b, kv, tiles):
        for r0, rr, c0, cc in tiles:
            same = qdoc_ref[r0:r0 + rr, :] == kdoc_ref[b:b + 1, c0:c0 + cc]
            if b == 0:
                rows = lax.broadcasted_iota(jnp.int32, (rr, cc), 0) + r0
                cols = lax.broadcasted_iota(jnp.int32, (rr, cc), 1) + c0
                same = same & (cols <= rows)
            bias_ref[r0:r0 + rr, c0:c0 + cc] = jnp.where(same, 0.0, -1e30)

        def head(h, carry):
            g = h // group
            qcol = pl.multiple_of(h * HD, HD)
            kcol = pl.multiple_of(g * HD, HD)
            vcol = pl.multiple_of(kv_width + g * HD, HD)
            for r0, rr, c0, cc in tiles:
                q = q_ref[r0:r0 + rr, pl.ds(qcol, HD)]
                keys = kv[c0:c0 + cc, pl.ds(kcol, HD)]
                values = kv[c0:c0 + cc, pl.ds(vcol, HD)]
                s = lax.dot_general(q, keys, (((1,), (1,)), ((), ())),
                                    preferred_element_type=jnp.float32) * scale
                s = s + bias_ref[r0:r0 + rr, c0:c0 + cc]
                prev = m_ref[h, r0:r0 + rr, :]
                top = jnp.max(s, axis=1, keepdims=True)
                best = jnp.maximum(prev, top)
                shrink = jnp.exp(prev - best)
                p = jnp.exp(s - best[:, :1])
                m_ref[h, r0:r0 + rr, :] = best
                l_ref[h, r0:r0 + rr, :] = l_ref[h, r0:r0 + rr, :] * shrink + jnp.sum(p, axis=1, keepdims=True)
                acc_ref[h, r0:r0 + rr, :] = acc_ref[h, r0:r0 + rr, :] * shrink + jnp.dot(
                    p.astype(jnp.bfloat16), values, preferred_element_type=jnp.float32)
            return carry

        lax.fori_loop(0, heads, head, 0)

    full = [(0, tok, 0, tok)]
    lower = [(0, half, 0, half), (half, half, 0, tok)]
    upper = [(0, half, 0, tok), (half, half, half, half)]
    nback = recv.shape[0]

    @pl.when(c < n - 1)
    def _():
        copy_of(0).start()

    compute(0, kv_ref, lower)
    for s in range(1, nback + 1):
        @pl.when(c >= s)
        def _():
            copy_of(s - 1).wait_recv()

        if s < nback:
            @pl.when(sends_at(s))
            def _():
                copy_of(s).start()

        @pl.when(c >= s)
        def _():
            compute(s, recv.at[s - 1], upper if s == nback else full)

    for s in range(nback):
        @pl.when(sends_at(s))
        def _():
            copy_of(s).wait_send()

    def finish(h, carry):
        col = pl.multiple_of(h * HD, HD)
        o_ref[:, pl.ds(col, HD)] = (acc_ref[h] / l_ref[h]).astype(o_ref.dtype)
        return carry

    lax.fori_loop(0, heads, finish, 0)


def ring_attention(queries, kv_local, qdoc, kdoc, kv_heads):
    tok, width = queries.shape
    group = width // HD // kv_heads
    heads = width // HD
    vmem = pltpu.VMEM
    return pl.pallas_call(
        functools.partial(ring_kernel, group, tok, HD ** (-0.5)),
        out_shape=jax.ShapeDtypeStruct((tok, width), queries.dtype),
        in_specs=[pl.BlockSpec(memory_space=vmem)] * 4,
        out_specs=pl.BlockSpec(memory_space=vmem),
        scratch_shapes=[
            vmem((CYCLE, tok, kv_local.shape[1]), kv_local.dtype),
            pltpu.SemaphoreType.DMA((CYCLE,)),
            pltpu.SemaphoreType.DMA((CYCLE,)),
            vmem((heads, tok, HD), jnp.float32),
            vmem((heads, tok, HD), jnp.float32),
            vmem((heads, tok, HD), jnp.float32),
            vmem((tok, tok), jnp.float32),
        ],
        compiler_params=pltpu.CompilerParams(
            collective_id=0, has_side_effects=True, vmem_limit_bytes=48 * 1024 * 1024),
    )(queries, kv_local, qdoc, kdoc)


def body(hidden, queries, lengths, norm_gain, kv_weight, kv_bias):
    tok, width = hidden.shape
    tpi = lax.axis_index("tp")
    across = flipped(hidden, "tp", 2)
    pair = flipped(jnp.stack([hidden, across]), "tp", 1)
    gain_across = flipped(norm_gain, "tp", 2)
    gain_pair = flipped(jnp.stack([norm_gain, gain_across]), "tp", 1)
    blocks = [
        (hidden, norm_gain, tpi),
        (across, gain_across, tpi ^ 2),
        (pair[0], gain_pair[0], tpi ^ 1),
        (pair[1], gain_pair[1], tpi ^ 3),
    ]
    squares = None
    for part, _, _ in blocks:
        xf = part.astype(jnp.float32)
        term = jnp.sum(xf * xf, axis=1)
        squares = term if squares is None else squares + term
    scale_rows = lax.rsqrt(squares / D + 1e-06)
    flat_weight = kv_weight.reshape(kv_weight.shape[0], -1)
    summed = None
    for part, gain, owner in blocks:
        normed = (part.astype(jnp.float32) * scale_rows[:, None] * gain[None, :]).astype(jnp.bfloat16)
        rows = lax.dynamic_slice_in_dim(flat_weight, owner * width, width, 0)
        term = jnp.dot(normed, rows, preferred_element_type=jnp.float32)
        summed = term if summed is None else summed + term
    kv_local = (summed + kv_bias.reshape(-1)[None, :]).astype(jnp.bfloat16)
    kv_heads = kv_weight.shape[2] // HD

    device = lax.axis_index("ctx")
    ends = jnp.cumsum(lengths)
    backs = jnp.arange(CYCLE + 1, dtype=jnp.int32)
    starts = (device - backs) * tok
    positions = starts[:, None] + jnp.arange(tok, dtype=jnp.int32)[None, :]
    found = jnp.sum((positions[:, :, None] >= ends[None, None, :]).astype(jnp.int32), axis=2)
    kdoc = jnp.where((device - backs >= 0)[:, None], found, -1)
    qdoc = found[0]
    kdoc = jnp.concatenate([kdoc, jnp.full((8 - CYCLE - 1, tok), -1, jnp.int32)], axis=0)
    return ring_attention(queries, kv_local, qdoc[:, None], kdoc, kv_heads)


def solution(mesh):
    in_specs = (P("ctx", "tp"), P("ctx", "tp"), P(), P("tp"), P(None, None, "tp"), P(None, "tp"))
    out_specs = P("ctx", "tp")
    return jax.shard_map(body, mesh=mesh, in_specs=in_specs, out_specs=out_specs, check_vma=False)
```

```python
import functools

import jax
import jax.numpy as jnp
from jax import lax
from jax.experimental import pallas as pl
from jax.experimental.pallas import tpu as pltpu
from jax.sharding import PartitionSpec as P

D = 5120
HD = 128
CYCLE = 4


def shifted(value, axis, steps):
    count = lax.axis_size(axis)
    leading, last = (max(0, -steps), min(count, count - steps))
    return lax.ppermute(value, axis, [(source, source + steps) for source in range(leading, last)])


def flipped(value, axis, bit):
    count = lax.axis_size(axis)
    return lax.ppermute(value, axis, [(source, source ^ bit) for source in range(count)])


def ring_kernel(group, tok, scale, q_ref, kv_ref, qdoc_ref, kdoc_ref, o_ref,
                recv, send_sem, recv_sem, m_ref, l_ref, acc_ref, bias_ref):
    c = lax.axis_index("ctx")
    t = lax.axis_index("tp")
    n = lax.axis_size("ctx")
    heads = q_ref.shape[1] // HD
    kv_width = kv_ref.shape[1] // 2
    half = tok // 2

    barrier = pltpu.get_barrier_semaphore()

    @pl.when(c > 0)
    def _():
        pl.semaphore_signal(barrier, inc=1, device_id=(c - 1, t), device_id_type=pl.DeviceIdType.MESH)

    @pl.when(c < n - 1)
    def _():
        pl.semaphore_signal(barrier, inc=1, device_id=(c + 1, t), device_id_type=pl.DeviceIdType.MESH)

    peers = (c > 0).astype(jnp.int32) + (c < n - 1).astype(jnp.int32)
    pl.semaphore_wait(barrier, peers)

    def copy_of(step):
        src = kv_ref if step == 0 else recv.at[step - 1]
        return pltpu.make_async_remote_copy(
            src_ref=src, dst_ref=recv.at[step], send_sem=send_sem.at[step],
            recv_sem=recv_sem.at[step], device_id=(c + 1, t),
            device_id_type=pl.DeviceIdType.MESH)

    def sends_at(step):
        return (c >= step) & (c < n - 1)

    m_ref[...] = jnp.full(m_ref.shape, -1e30, jnp.float32)
    l_ref[...] = jnp.zeros(l_ref.shape, jnp.float32)
    acc_ref[...] = jnp.zeros(acc_ref.shape, jnp.float32)

    def compute(b, kv, tiles):
        for r0, rr, c0, cc in tiles:
            same = qdoc_ref[r0:r0 + rr, :] == kdoc_ref[b:b + 1, c0:c0 + cc]
            if b == 0:
                rows = lax.broadcasted_iota(jnp.int32, (rr, cc), 0) + r0
                cols = lax.broadcasted_iota(jnp.int32, (rr, cc), 1) + c0
                same = same & (cols <= rows)
            bias_ref[r0:r0 + rr, c0:c0 + cc] = jnp.where(same, 0.0, -1e30)

        def pair_of_heads(g, carry):
            kcol = pl.multiple_of(g * HD, HD)
            vcol = pl.multiple_of(kv_width + g * HD, HD)
            for j in range(group):
                h = g * group + j
                qcol = pl.multiple_of(h * HD, HD)
                for r0, rr, c0, cc in tiles:
                    q = q_ref[r0:r0 + rr, pl.ds(qcol, HD)]
                    keys = kv[c0:c0 + cc, pl.ds(kcol, HD)]
                    values = kv[c0:c0 + cc, pl.ds(vcol, HD)]
                    s = lax.dot_general(q, keys, (((1,), (1,)), ((), ())),
                                        preferred_element_type=jnp.float32) * scale
                    s = s + bias_ref[r0:r0 + rr, c0:c0 + cc]
                    prev = m_ref[h, r0:r0 + rr, :]
                    top = jnp.max(s, axis=1, keepdims=True)
                    best = jnp.maximum(prev, top)
                    shrink = jnp.exp(prev - best)
                    p = jnp.exp(s - best[:, :1])
                    m_ref[h, r0:r0 + rr, :] = best
                    l_ref[h, r0:r0 + rr, :] = l_ref[h, r0:r0 + rr, :] * shrink + jnp.sum(p, axis=1, keepdims=True)
                    acc_ref[h, r0:r0 + rr, :] = acc_ref[h, r0:r0 + rr, :] * shrink + jnp.dot(
                        p.astype(jnp.bfloat16), values, preferred_element_type=jnp.float32)
            return carry

        lax.fori_loop(0, heads // group, pair_of_heads, 0)

    full = [(0, tok, 0, tok)]
    lower = [(0, half, 0, half), (half, half, 0, tok)]
    upper = [(0, half, 0, tok), (half, half, half, half)]
    nback = recv.shape[0]

    @pl.when(c < n - 1)
    def _():
        copy_of(0).start()

    compute(0, kv_ref, lower)
    for s in range(1, nback + 1):
        @pl.when(c >= s)
        def _():
            copy_of(s - 1).wait_recv()

        if s < nback:
            @pl.when(sends_at(s))
            def _():
                copy_of(s).start()

        @pl.when(c >= s)
        def _():
            compute(s, recv.at[s - 1], upper if s == nback else full)

    for s in range(nback):
        @pl.when(sends_at(s))
        def _():
            copy_of(s).wait_send()

    def finish(h, carry):
        col = pl.multiple_of(h * HD, HD)
        o_ref[:, pl.ds(col, HD)] = (acc_ref[h] / l_ref[h]).astype(o_ref.dtype)
        return carry

    lax.fori_loop(0, heads, finish, 0)


def ring_attention(queries, kv_local, qdoc, kdoc, kv_heads):
    tok, width = queries.shape
    group = width // HD // kv_heads
    heads = width // HD
    vmem = pltpu.VMEM
    return pl.pallas_call(
        functools.partial(ring_kernel, group, tok, HD ** (-0.5)),
        out_shape=jax.ShapeDtypeStruct((tok, width), queries.dtype),
        in_specs=[pl.BlockSpec(memory_space=vmem)] * 4,
        out_specs=pl.BlockSpec(memory_space=vmem),
        scratch_shapes=[
            vmem((CYCLE, tok, kv_local.shape[1]), kv_local.dtype),
            pltpu.SemaphoreType.DMA((CYCLE,)),
            pltpu.SemaphoreType.DMA((CYCLE,)),
            vmem((heads, tok, HD), jnp.float32),
            vmem((heads, tok, HD), jnp.float32),
            vmem((heads, tok, HD), jnp.float32),
            vmem((tok, tok), jnp.float32),
        ],
        compiler_params=pltpu.CompilerParams(
            collective_id=0, has_side_effects=True, vmem_limit_bytes=48 * 1024 * 1024),
    )(queries, kv_local, qdoc, kdoc)


def body(hidden, queries, lengths, norm_gain, kv_weight, kv_bias):
    tok, width = hidden.shape
    tpi = lax.axis_index("tp")
    across = flipped(hidden, "tp", 2)
    beside = flipped(hidden, "tp", 1)
    diagonal = flipped(across, "tp", 1)
    gain_across = flipped(norm_gain, "tp", 2)
    gain_beside = flipped(norm_gain, "tp", 1)
    gain_diagonal = flipped(gain_across, "tp", 1)
    blocks = [
        (hidden, norm_gain, tpi),
        (across, gain_across, tpi ^ 2),
        (beside, gain_beside, tpi ^ 1),
        (diagonal, gain_diagonal, tpi ^ 3),
    ]
    squares = None
    for part, _, _ in blocks:
        xf = part.astype(jnp.float32)
        term = jnp.sum(xf * xf, axis=1)
        squares = term if squares is None else squares + term
    scale_rows = lax.rsqrt(squares / D + 1e-06)
    flat_weight = kv_weight.reshape(kv_weight.shape[0], -1)
    summed = None
    for part, gain, owner in blocks:
        normed = (part.astype(jnp.float32) * scale_rows[:, None] * gain[None, :]).astype(jnp.bfloat16)
        rows = lax.dynamic_slice_in_dim(flat_weight, owner * width, width, 0)
        term = jnp.dot(normed, rows, preferred_element_type=jnp.float32)
        summed = term if summed is None else summed + term
    kv_local = (summed + kv_bias.reshape(-1)[None, :]).astype(jnp.bfloat16)
    kv_heads = kv_weight.shape[2] // HD

    device = lax.axis_index("ctx")
    ends = jnp.cumsum(lengths)
    backs = jnp.arange(CYCLE + 1, dtype=jnp.int32)
    starts = (device - backs) * tok
    positions = starts[:, None] + jnp.arange(tok, dtype=jnp.int32)[None, :]
    found = jnp.sum((positions[:, :, None] >= ends[None, None, :]).astype(jnp.int32), axis=2)
    kdoc = jnp.where((device - backs >= 0)[:, None], found, -1)
    qdoc = found[0]
    kdoc = jnp.concatenate([kdoc, jnp.full((8 - CYCLE - 1, tok), -1, jnp.int32)], axis=0)
    return ring_attention(queries, kv_local, qdoc[:, None], kdoc, kv_heads)


def solution(mesh):
    in_specs = (P("ctx", "tp"), P("ctx", "tp"), P(), P("tp"), P(None, None, "tp"), P(None, "tp"))
    out_specs = P("ctx", "tp")
    return jax.shard_map(body, mesh=mesh, in_specs=in_specs, out_specs=out_specs, check_vma=False)
```

```python
import functools

import jax
import jax.numpy as jnp
from jax import lax
from jax.experimental import pallas as pl
from jax.experimental.pallas import tpu as pltpu
from jax.sharding import PartitionSpec as P

D = 5120
HD = 128
CYCLE = 4


def shifted(value, axis, steps):
    count = lax.axis_size(axis)
    leading, last = (max(0, -steps), min(count, count - steps))
    return lax.ppermute(value, axis, [(source, source + steps) for source in range(leading, last)])


def flipped(value, axis, bit):
    count = lax.axis_size(axis)
    return lax.ppermute(value, axis, [(source, source ^ bit) for source in range(count)])


def ring_kernel(group, tok, scale, q_ref, kv_ref, qdoc_ref, kdoc_ref, o_ref,
                recv, send_sem, recv_sem, m_ref, l_ref, acc_ref, bias_ref):
    c = lax.axis_index("ctx")
    t = lax.axis_index("tp")
    n = lax.axis_size("ctx")
    heads = q_ref.shape[1] // HD
    kv_width = kv_ref.shape[1] // 2
    half = tok // 2

    barrier = pltpu.get_barrier_semaphore()

    @pl.when(c > 0)
    def _():
        pl.semaphore_signal(barrier, inc=1, device_id=(c - 1, t), device_id_type=pl.DeviceIdType.MESH)

    @pl.when(c < n - 1)
    def _():
        pl.semaphore_signal(barrier, inc=1, device_id=(c + 1, t), device_id_type=pl.DeviceIdType.MESH)

    peers = (c > 0).astype(jnp.int32) + (c < n - 1).astype(jnp.int32)
    pl.semaphore_wait(barrier, peers)

    def copy_of(step):
        src = kv_ref if step == 0 else recv.at[step - 1]
        return pltpu.make_async_remote_copy(
            src_ref=src, dst_ref=recv.at[step], send_sem=send_sem.at[step],
            recv_sem=recv_sem.at[step], device_id=(c + 1, t),
            device_id_type=pl.DeviceIdType.MESH)

    def sends_at(step):
        return (c >= step) & (c < n - 1)

    m_ref[...] = jnp.full(m_ref.shape, -1e30, jnp.float32)
    l_ref[...] = jnp.zeros(l_ref.shape, jnp.float32)
    acc_ref[...] = jnp.zeros(acc_ref.shape, jnp.float32)

    def compute(b, kv, tiles):
        for r0, rr, c0, cc in tiles:
            same = qdoc_ref[r0:r0 + rr, :] == kdoc_ref[b:b + 1, c0:c0 + cc]
            if b == 0:
                rows = lax.broadcasted_iota(jnp.int32, (rr, cc), 0) + r0
                cols = lax.broadcasted_iota(jnp.int32, (rr, cc), 1) + c0
                same = same & (cols <= rows)
            bias_ref[r0:r0 + rr, c0:c0 + cc] = jnp.where(same, 0.0, -1e30)

        def pair_of_heads(g, carry):
            kcol = pl.multiple_of(g * HD, HD)
            vcol = pl.multiple_of(kv_width + g * HD, HD)
            for j in range(group):
                h = g * group + j
                qcol = pl.multiple_of(h * HD, HD)
                for r0, rr, c0, cc in tiles:
                    q = q_ref[r0:r0 + rr, pl.ds(qcol, HD)]
                    keys = kv[c0:c0 + cc, pl.ds(kcol, HD)]
                    values = kv[c0:c0 + cc, pl.ds(vcol, HD)]
                    s = lax.dot_general(q, keys, (((1,), (1,)), ((), ())),
                                        preferred_element_type=jnp.float32) * scale
                    s = s + bias_ref[r0:r0 + rr, c0:c0 + cc]
                    prev = m_ref[h, r0:r0 + rr, :]
                    top = jnp.max(s, axis=1, keepdims=True)
                    best = jnp.maximum(prev, top)
                    shrink = jnp.exp(prev - best)
                    p = jnp.exp(s - best[:, :1])
                    m_ref[h, r0:r0 + rr, :] = best
                    l_ref[h, r0:r0 + rr, :] = l_ref[h, r0:r0 + rr, :] * shrink + jnp.sum(p, axis=1, keepdims=True)
                    acc_ref[h, r0:r0 + rr, :] = acc_ref[h, r0:r0 + rr, :] * shrink + jnp.dot(
                        p.astype(jnp.bfloat16), values, preferred_element_type=jnp.float32)
            return carry

        lax.fori_loop(0, heads // group, pair_of_heads, 0)

    full = [(0, tok, 0, tok)]
    lower = [(0, half, 0, half), (half, half, 0, tok)]
    upper = [(0, half, 0, tok), (half, half, half, half)]
    nback = recv.shape[0]

    @pl.when(c < n - 1)
    def _():
        copy_of(0).start()

    compute(0, kv_ref, lower)
    for s in range(1, nback + 1):
        @pl.when(c >= s)
        def _():
            copy_of(s - 1).wait_recv()

        if s < nback:
            @pl.when(sends_at(s))
            def _():
                copy_of(s).start()

        @pl.when(c >= s)
        def _():
            compute(s, recv.at[s - 1], upper if s == nback else full)

    for s in range(nback):
        @pl.when(sends_at(s))
        def _():
            copy_of(s).wait_send()

    def finish(h, carry):
        col = pl.multiple_of(h * HD, HD)
        o_ref[:, pl.ds(col, HD)] = (acc_ref[h] / l_ref[h]).astype(o_ref.dtype)
        return carry

    lax.fori_loop(0, heads, finish, 0)


def ring_attention(queries, kv_local, qdoc, kdoc, kv_heads):
    tok, width = queries.shape
    group = width // HD // kv_heads
    heads = width // HD
    vmem = pltpu.VMEM
    return pl.pallas_call(
        functools.partial(ring_kernel, group, tok, HD ** (-0.5)),
        out_shape=jax.ShapeDtypeStruct((tok, width), queries.dtype),
        in_specs=[pl.BlockSpec(memory_space=vmem)] * 4,
        out_specs=pl.BlockSpec(memory_space=vmem),
        scratch_shapes=[
            vmem((CYCLE, tok, kv_local.shape[1]), kv_local.dtype),
            pltpu.SemaphoreType.DMA((CYCLE,)),
            pltpu.SemaphoreType.DMA((CYCLE,)),
            vmem((heads, tok, HD), jnp.float32),
            vmem((heads, tok, HD), jnp.float32),
            vmem((heads, tok, HD), jnp.float32),
            vmem((tok, tok), jnp.float32),
        ],
        compiler_params=pltpu.CompilerParams(
            collective_id=0, has_side_effects=True, vmem_limit_bytes=48 * 1024 * 1024),
    )(queries, kv_local, qdoc, kdoc)


def body(hidden, queries, lengths, norm_gain, kv_weight, kv_bias):
    tok, width = hidden.shape
    tpi = lax.axis_index("tp")
    own_squares = jnp.sum(jnp.square(hidden.astype(jnp.float32)), axis=1)
    squares_across = flipped(own_squares, "tp", 2)
    squares_beside = flipped(own_squares, "tp", 1)
    squares_diagonal = flipped(squares_across, "tp", 1)
    squares = own_squares + squares_beside + squares_across + squares_diagonal
    scale_rows = lax.rsqrt(squares / D + 1e-06)
    sending, _ = lax.optimization_barrier((hidden, squares_across))
    across = flipped(sending, "tp", 2)
    beside = flipped(hidden, "tp", 1)
    gain_across = flipped(norm_gain, "tp", 2)
    gain_beside = flipped(norm_gain, "tp", 1)
    gain_diagonal = flipped(gain_across, "tp", 1)
    flat_weight = kv_weight.reshape(kv_weight.shape[0], -1)

    def project(part, gain, owner):
        normed = (part.astype(jnp.float32) * scale_rows[:, None] * gain[None, :]).astype(jnp.bfloat16)
        rows = lax.dynamic_slice_in_dim(flat_weight, owner * width, width, 0)
        return jnp.dot(normed, rows, preferred_element_type=jnp.float32)

    summed = project(hidden, norm_gain, tpi) + project(beside, gain_beside, tpi ^ 1)
    across, summed = lax.optimization_barrier((across, summed))
    diagonal = flipped(across, "tp", 1)
    summed = summed + project(across, gain_across, tpi ^ 2)
    summed = summed + project(diagonal, gain_diagonal, tpi ^ 3)
    kv_local = (summed + kv_bias.reshape(-1)[None, :]).astype(jnp.bfloat16)
    kv_heads = kv_weight.shape[2] // HD

    device = lax.axis_index("ctx")
    ends = jnp.cumsum(lengths)
    backs = jnp.arange(CYCLE + 1, dtype=jnp.int32)
    starts = (device - backs) * tok
    positions = starts[:, None] + jnp.arange(tok, dtype=jnp.int32)[None, :]
    found = jnp.sum((positions[:, :, None] >= ends[None, None, :]).astype(jnp.int32), axis=2)
    kdoc = jnp.where((device - backs >= 0)[:, None], found, -1)
    qdoc = found[0]
    kdoc = jnp.concatenate([kdoc, jnp.full((8 - CYCLE - 1, tok), -1, jnp.int32)], axis=0)
    return ring_attention(queries, kv_local, qdoc[:, None], kdoc, kv_heads)


def solution(mesh):
    in_specs = (P("ctx", "tp"), P("ctx", "tp"), P(), P("tp"), P(None, None, "tp"), P(None, "tp"))
    out_specs = P("ctx", "tp")
    return jax.shard_map(body, mesh=mesh, in_specs=in_specs, out_specs=out_specs, check_vma=False)
```

```python
import functools

import jax
import jax.numpy as jnp
from jax import lax
from jax.experimental import pallas as pl
from jax.experimental.pallas import tpu as pltpu
from jax.sharding import PartitionSpec as P

D = 5120
HD = 128
CYCLE = 4


def shifted(value, axis, steps):
    count = lax.axis_size(axis)
    leading, last = (max(0, -steps), min(count, count - steps))
    return lax.ppermute(value, axis, [(source, source + steps) for source in range(leading, last)])


def flipped(value, axis, bit):
    count = lax.axis_size(axis)
    return lax.ppermute(value, axis, [(source, source ^ bit) for source in range(count)])


def ring_kernel(group, scale, key_half, first, final, q_ref, kv_ref, qdoc_ref, kdoc_ref, *rest):
    if first:
        (out_m, out_l, out_acc, recv, send_sem, recv_sem, m_ref, l_ref, acc_ref, bias_ref) = rest
    else:
        (in_m, in_l, in_acc, o_ref, recv, send_sem, recv_sem, m_ref, l_ref, acc_ref, bias_ref) = rest
    c = lax.axis_index("ctx")
    t = lax.axis_index("tp")
    n = lax.axis_size("ctx")
    tok = q_ref.shape[0]
    keys_n = kv_ref.shape[0]
    heads = q_ref.shape[1] // HD
    kv_width = kv_ref.shape[1] // 2
    key_base = key_half * keys_n

    barrier = pltpu.get_barrier_semaphore()

    @pl.when(c > 0)
    def _():
        pl.semaphore_signal(barrier, inc=1, device_id=(c - 1, t), device_id_type=pl.DeviceIdType.MESH)

    @pl.when(c < n - 1)
    def _():
        pl.semaphore_signal(barrier, inc=1, device_id=(c + 1, t), device_id_type=pl.DeviceIdType.MESH)

    peers = (c > 0).astype(jnp.int32) + (c < n - 1).astype(jnp.int32)
    pl.semaphore_wait(barrier, peers)

    def copy_of(step):
        src = kv_ref if step == 0 else recv.at[step - 1]
        return pltpu.make_async_remote_copy(
            src_ref=src, dst_ref=recv.at[step], send_sem=send_sem.at[step],
            recv_sem=recv_sem.at[step], device_id=(c + 1, t),
            device_id_type=pl.DeviceIdType.MESH)

    def sends_at(step):
        return (c >= step) & (c < n - 1)

    @pl.when(c < n - 1)
    def _():
        copy_of(0).start()

    if first:
        m_ref[...] = jnp.full(m_ref.shape, -1e30, jnp.float32)
        l_ref[...] = jnp.zeros(l_ref.shape, jnp.float32)
        acc_ref[...] = jnp.zeros(acc_ref.shape, jnp.float32)
    else:
        m_ref[...] = in_m[...]
        l_ref[...] = in_l[...]
        acc_ref[...] = in_acc[...]

    def compute(b, kv, tiles):
        for r0, rr, c0, cc in tiles:
            same = qdoc_ref[r0:r0 + rr, :] == kdoc_ref[b:b + 1, c0:c0 + cc]
            if b == 0:
                rows = lax.broadcasted_iota(jnp.int32, (rr, cc), 0) + r0
                cols = lax.broadcasted_iota(jnp.int32, (rr, cc), 1) + (c0 + key_base)
                same = same & (cols <= rows)
            bias_ref[r0:r0 + rr, c0:c0 + cc] = jnp.where(same, 0.0, -1e30)

        def head(h, carry):
            g = h // group
            qcol = pl.multiple_of(h * HD, HD)
            kcol = pl.multiple_of(g * HD, HD)
            vcol = pl.multiple_of(kv_width + g * HD, HD)
            for r0, rr, c0, cc in tiles:
                q = q_ref[r0:r0 + rr, pl.ds(qcol, HD)]
                keys = kv[c0:c0 + cc, pl.ds(kcol, HD)]
                values = kv[c0:c0 + cc, pl.ds(vcol, HD)]
                s = lax.dot_general(q, keys, (((1,), (1,)), ((), ())),
                                    preferred_element_type=jnp.float32) * scale
                s = s + bias_ref[r0:r0 + rr, c0:c0 + cc]
                prev = m_ref[h, r0:r0 + rr, :]
                top = jnp.max(s, axis=1, keepdims=True)
                best = jnp.maximum(prev, top)
                shrink = jnp.exp(prev - best)
                p = jnp.exp(s - best[:, :1])
                m_ref[h, r0:r0 + rr, :] = best
                l_ref[h, r0:r0 + rr, :] = l_ref[h, r0:r0 + rr, :] * shrink + jnp.sum(p, axis=1, keepdims=True)
                acc_ref[h, r0:r0 + rr, :] = acc_ref[h, r0:r0 + rr, :] * shrink + jnp.dot(
                    p.astype(jnp.bfloat16), values, preferred_element_type=jnp.float32)
            return carry

        lax.fori_loop(0, heads, head, 0)

    lead = tok - keys_n
    if key_half == 0:
        own = [(0, keys_n, 0, keys_n), (keys_n, lead, 0, keys_n)]
        oldest = [(0, keys_n, 0, keys_n)]
    else:
        own = [(key_base, keys_n, 0, keys_n)]
        oldest = [(0, tok, 0, keys_n)]
    nback = recv.shape[0]

    compute(0, kv_ref, own)
    for s in range(1, nback + 1):
        @pl.when(c >= s)
        def _():
            copy_of(s - 1).wait_recv()

        if s < nback:
            @pl.when(sends_at(s))
            def _():
                copy_of(s).start()

        @pl.when(c >= s)
        def _():
            compute(s, recv.at[s - 1], oldest if s == nback else [(0, tok, 0, keys_n)])

    for s in range(nback):
        @pl.when(sends_at(s))
        def _():
            copy_of(s).wait_send()

    if first:
        out_m[...] = m_ref[...]
        out_l[...] = l_ref[...]
        out_acc[...] = acc_ref[...]
    else:
        def finish(h, carry):
            col = pl.multiple_of(h * HD, HD)
            o_ref[:, pl.ds(col, HD)] = (acc_ref[h] / l_ref[h]).astype(o_ref.dtype)
            return carry

        lax.fori_loop(0, heads, finish, 0)


def ring_attention(queries, kv_half, qdoc, kdoc, kv_heads, key_half, state=None):
    tok, width = queries.shape
    group = width // HD // kv_heads
    heads = width // HD
    first = state is None
    vmem = pltpu.VMEM
    stat = jax.ShapeDtypeStruct((heads, tok, HD), jnp.float32)
    if first:
        out_shape = (stat, stat, stat)
        out_specs = (pl.BlockSpec(memory_space=vmem),) * 3
        operands = (queries, kv_half, qdoc, kdoc)
    else:
        out_shape = jax.ShapeDtypeStruct((tok, width), queries.dtype)
        out_specs = pl.BlockSpec(memory_space=vmem)
        operands = (queries, kv_half, qdoc, kdoc) + tuple(state)
    return pl.pallas_call(
        functools.partial(ring_kernel, group, HD ** (-0.5), key_half, first, not first),
        out_shape=out_shape,
        in_specs=[pl.BlockSpec(memory_space=vmem)] * len(operands),
        out_specs=out_specs,
        scratch_shapes=[
            vmem((CYCLE,) + kv_half.shape, kv_half.dtype),
            pltpu.SemaphoreType.DMA((CYCLE,)),
            pltpu.SemaphoreType.DMA((CYCLE,)),
            vmem((heads, tok, HD), jnp.float32),
            vmem((heads, tok, HD), jnp.float32),
            vmem((heads, tok, HD), jnp.float32),
            vmem((tok, kv_half.shape[0]), jnp.float32),
        ],
        compiler_params=pltpu.CompilerParams(
            collective_id=key_half, has_side_effects=True, vmem_limit_bytes=56 * 1024 * 1024),
    )(*operands)


def body(hidden, queries, lengths, norm_gain, kv_weight, kv_bias):
    tok, width = hidden.shape
    tpi = lax.axis_index("tp")
    own_squares = jnp.sum(jnp.square(hidden.astype(jnp.float32)), axis=1)
    squares_across = flipped(own_squares, "tp", 2)
    squares_beside = flipped(own_squares, "tp", 1)
    squares_diagonal = flipped(squares_across, "tp", 1)
    squares = own_squares + squares_beside + squares_across + squares_diagonal
    scale_rows = lax.rsqrt(squares / D + 1e-06)
    half = tok // 2
    sending, _ = lax.optimization_barrier((hidden[:half], squares_across))
    across_a = flipped(sending, "tp", 2)
    beside = flipped(hidden, "tp", 1)
    gain_across = flipped(norm_gain, "tp", 2)
    gain_beside = flipped(norm_gain, "tp", 1)
    gain_diagonal = flipped(gain_across, "tp", 1)
    flat_weight = kv_weight.reshape(kv_weight.shape[0], -1)
    bias = kv_bias.reshape(-1)[None, :]

    def project(part, gain, owner, scale):
        normed = (part.astype(jnp.float32) * scale[:, None] * gain[None, :]).astype(jnp.bfloat16)
        rows = lax.dynamic_slice_in_dim(flat_weight, owner * width, width, 0)
        return jnp.dot(normed, rows, preferred_element_type=jnp.float32)

    summed = project(hidden, norm_gain, tpi, scale_rows) + project(beside, gain_beside, tpi ^ 1, scale_rows)
    across_a, summed = lax.optimization_barrier((across_a, summed))
    sending, _ = lax.optimization_barrier((hidden[half:], across_a))
    across_b = flipped(sending, "tp", 2)
    diagonal_a = flipped(across_a, "tp", 1)
    kv_a = (summed[:half] + project(across_a, gain_across, tpi ^ 2, scale_rows[:half])
            + project(diagonal_a, gain_diagonal, tpi ^ 3, scale_rows[:half]) + bias).astype(jnp.bfloat16)
    kv_heads = kv_weight.shape[2] // HD

    device = lax.axis_index("ctx")
    ends = jnp.cumsum(lengths)
    backs = jnp.arange(CYCLE + 1, dtype=jnp.int32)
    starts = (device - backs) * tok
    positions = starts[:, None] + jnp.arange(tok, dtype=jnp.int32)[None, :]
    found = jnp.sum((positions[:, :, None] >= ends[None, None, :]).astype(jnp.int32), axis=2)
    kdoc = jnp.where((device - backs >= 0)[:, None], found, -1)
    qdoc = found[0][:, None]
    kdoc = jnp.concatenate([kdoc, jnp.full((8 - CYCLE - 1, tok), -1, jnp.int32)], axis=0)

    state = ring_attention(queries, kv_a, qdoc, kdoc[:, :half], kv_heads, 0)
    across_b, state = lax.optimization_barrier((across_b, state))
    diagonal_b = flipped(across_b, "tp", 1)
    kv_b = (summed[half:] + project(across_b, gain_across, tpi ^ 2, scale_rows[half:])
            + project(diagonal_b, gain_diagonal, tpi ^ 3, scale_rows[half:]) + bias).astype(jnp.bfloat16)
    return ring_attention(queries, kv_b, qdoc, kdoc[:, half:], kv_heads, 1, state)


def solution(mesh):
    in_specs = (P("ctx", "tp"), P("ctx", "tp"), P(), P("tp"), P(None, None, "tp"), P(None, "tp"))
    out_specs = P("ctx", "tp")
    return jax.shard_map(body, mesh=mesh, in_specs=in_specs, out_specs=out_specs, check_vma=False)
```

```python
import functools

import jax
import jax.numpy as jnp
from jax import lax
from jax.experimental import pallas as pl
from jax.experimental.pallas import tpu as pltpu
from jax.sharding import PartitionSpec as P

D = 5120
HD = 128
CYCLE = 4


def shifted(value, axis, steps):
    count = lax.axis_size(axis)
    leading, last = (max(0, -steps), min(count, count - steps))
    return lax.ppermute(value, axis, [(source, source + steps) for source in range(leading, last)])


def flipped(value, axis, bit):
    count = lax.axis_size(axis)
    return lax.ppermute(value, axis, [(source, source ^ bit) for source in range(count)])


def ring_kernel(group, tok, scale, q_ref, kv_ref, qdoc_ref, kdoc_ref, o_ref,
                recv, send_sem, recv_sem, m_ref, l_ref, acc_ref, bias_ref):
    c = lax.axis_index("ctx")
    t = lax.axis_index("tp")
    n = lax.axis_size("ctx")
    heads = q_ref.shape[1] // HD
    kv_width = kv_ref.shape[1] // 2
    half = tok // 2

    barrier = pltpu.get_barrier_semaphore()

    @pl.when(c > 0)
    def _():
        pl.semaphore_signal(barrier, inc=1, device_id=(c - 1, t), device_id_type=pl.DeviceIdType.MESH)

    @pl.when(c < n - 1)
    def _():
        pl.semaphore_signal(barrier, inc=1, device_id=(c + 1, t), device_id_type=pl.DeviceIdType.MESH)

    peers = (c > 0).astype(jnp.int32) + (c < n - 1).astype(jnp.int32)
    pl.semaphore_wait(barrier, peers)

    def copy_of(step):
        src = kv_ref if step == 0 else recv.at[step - 1]
        return pltpu.make_async_remote_copy(
            src_ref=src, dst_ref=recv.at[step], send_sem=send_sem.at[step],
            recv_sem=recv_sem.at[step], device_id=(c + 1, t),
            device_id_type=pl.DeviceIdType.MESH)

    def sends_at(step):
        return (c >= step) & (c < n - 1)

    m_ref[...] = jnp.full(m_ref.shape, -1e30, jnp.float32)
    l_ref[...] = jnp.zeros(l_ref.shape, jnp.float32)
    acc_ref[...] = jnp.zeros(acc_ref.shape, jnp.float32)

    def compute(b, kv, tiles):
        for r0, rr, c0, cc in tiles:
            same = qdoc_ref[r0:r0 + rr, :] == kdoc_ref[b:b + 1, c0:c0 + cc]
            if b == 0:
                rows = lax.broadcasted_iota(jnp.int32, (rr, cc), 0) + r0
                cols = lax.broadcasted_iota(jnp.int32, (rr, cc), 1) + c0
                same = same & (cols <= rows)
            bias_ref[r0:r0 + rr, c0:c0 + cc] = jnp.where(same, 0.0, -1e30)

        def pair_of_heads(g, carry):
            kcol = pl.multiple_of(g * HD, HD)
            vcol = pl.multiple_of(kv_width + g * HD, HD)
            for j in range(group):
                h = g * group + j
                qcol = pl.multiple_of(h * HD, HD)
                for r0, rr, c0, cc in tiles:
                    q = q_ref[r0:r0 + rr, pl.ds(qcol, HD)]
                    keys = kv[c0:c0 + cc, pl.ds(kcol, HD)]
                    values = kv[c0:c0 + cc, pl.ds(vcol, HD)]
                    s = lax.dot_general(q, keys, (((1,), (1,)), ((), ())),
                                        preferred_element_type=jnp.float32) * scale
                    s = s + bias_ref[r0:r0 + rr, c0:c0 + cc]
                    prev = m_ref[h, r0:r0 + rr, :]
                    top = jnp.max(s, axis=1, keepdims=True)
                    best = jnp.maximum(prev, top)
                    shrink = jnp.exp(prev - best)
                    p = jnp.exp(s - best[:, :1])
                    m_ref[h, r0:r0 + rr, :] = best
                    l_ref[h, r0:r0 + rr, :] = l_ref[h, r0:r0 + rr, :] * shrink + jnp.sum(p, axis=1, keepdims=True)
                    acc_ref[h, r0:r0 + rr, :] = acc_ref[h, r0:r0 + rr, :] * shrink + jnp.dot(
                        p.astype(jnp.bfloat16), values, preferred_element_type=jnp.float32)
            return carry

        lax.fori_loop(0, heads // group, pair_of_heads, 0)

    full = [(0, tok, 0, tok)]
    lower = [(0, half, 0, half), (half, half, 0, tok)]
    upper = [(0, half, 0, tok), (half, half, half, half)]
    nback = recv.shape[0]

    @pl.when(c < n - 1)
    def _():
        copy_of(0).start()

    compute(0, kv_ref, lower)
    for s in range(1, nback + 1):
        @pl.when(c >= s)
        def _():
            copy_of(s - 1).wait_recv()

        if s < nback:
            @pl.when(sends_at(s))
            def _():
                copy_of(s).start()

        @pl.when(c >= s)
        def _():
            compute(s, recv.at[s - 1], upper if s == nback else full)

    for s in range(nback):
        @pl.when(sends_at(s))
        def _():
            copy_of(s).wait_send()

    def finish(h, carry):
        col = pl.multiple_of(h * HD, HD)
        o_ref[:, pl.ds(col, HD)] = (acc_ref[h] / l_ref[h]).astype(o_ref.dtype)
        return carry

    lax.fori_loop(0, heads, finish, 0)


def ring_attention(queries, kv_local, qdoc, kdoc, kv_heads):
    tok, width = queries.shape
    group = width // HD // kv_heads
    heads = width // HD
    vmem = pltpu.VMEM
    return pl.pallas_call(
        functools.partial(ring_kernel, group, tok, HD ** (-0.5)),
        out_shape=jax.ShapeDtypeStruct((tok, width), queries.dtype),
        in_specs=[pl.BlockSpec(memory_space=vmem)] * 4,
        out_specs=pl.BlockSpec(memory_space=vmem),
        scratch_shapes=[
            vmem((CYCLE, tok, kv_local.shape[1]), kv_local.dtype),
            pltpu.SemaphoreType.DMA((CYCLE,)),
            pltpu.SemaphoreType.DMA((CYCLE,)),
            vmem((heads, tok, HD), jnp.float32),
            vmem((heads, tok, HD), jnp.float32),
            vmem((heads, tok, HD), jnp.float32),
            vmem((tok, tok), jnp.float32),
        ],
        compiler_params=pltpu.CompilerParams(
            collective_id=0, has_side_effects=True, vmem_limit_bytes=48 * 1024 * 1024),
    )(queries, kv_local, qdoc, kdoc)


def body(hidden, queries, lengths, norm_gain, kv_weight, kv_bias):
    tok, width = hidden.shape
    tpi = lax.axis_index("tp")
    across = flipped(hidden, "tp", 2)
    own_squares = jnp.sum(jnp.square(hidden.astype(jnp.float32)), axis=1)
    squares_diagonal = flipped(own_squares, "tp", 3)
    squares_beside = flipped(own_squares, "tp", 1)
    squares_across = flipped(squares_diagonal, "tp", 1)
    squares = own_squares + squares_beside + squares_across + squares_diagonal
    scale_rows = lax.rsqrt(squares / D + 1e-06)
    beside = flipped(hidden, "tp", 1)
    gain_across = flipped(norm_gain, "tp", 2)
    gain_beside = flipped(norm_gain, "tp", 1)
    gain_diagonal = flipped(gain_across, "tp", 1)
    flat_weight = kv_weight.reshape(kv_weight.shape[0], -1)

    def project(part, gain, owner):
        normed = (part.astype(jnp.float32) * scale_rows[:, None] * gain[None, :]).astype(jnp.bfloat16)
        rows = lax.dynamic_slice_in_dim(flat_weight, owner * width, width, 0)
        return jnp.dot(normed, rows, preferred_element_type=jnp.float32)

    device = lax.axis_index("ctx")
    ends = jnp.cumsum(lengths)
    backs = jnp.arange(CYCLE + 1, dtype=jnp.int32)
    starts = (device - backs) * tok
    positions = starts[:, None] + jnp.arange(tok, dtype=jnp.int32)[None, :]
    found = jnp.sum((positions[:, :, None] >= ends[None, None, :]).astype(jnp.int32), axis=2)
    kdoc = jnp.where((device - backs >= 0)[:, None], found, -1)
    qdoc = found[0]
    kdoc = jnp.concatenate([kdoc, jnp.full((8 - CYCLE - 1, tok), -1, jnp.int32)], axis=0)

    summed = project(hidden, norm_gain, tpi) + project(beside, gain_beside, tpi ^ 1)
    across, summed, qdoc, kdoc = lax.optimization_barrier((across, summed, qdoc, kdoc))
    diagonal = flipped(across, "tp", 1)
    summed = summed + project(across, gain_across, tpi ^ 2)
    summed = summed + project(diagonal, gain_diagonal, tpi ^ 3)
    kv_local = (summed + kv_bias.reshape(-1)[None, :]).astype(jnp.bfloat16)
    kv_heads = kv_weight.shape[2] // HD

    return ring_attention(queries, kv_local, qdoc[:, None], kdoc, kv_heads)


def solution(mesh):
    in_specs = (P("ctx", "tp"), P("ctx", "tp"), P(), P("tp"), P(None, None, "tp"), P(None, "tp"))
    out_specs = P("ctx", "tp")
    return jax.shard_map(body, mesh=mesh, in_specs=in_specs, out_specs=out_specs, check_vma=False)
```

```python
import functools

import jax
import jax.numpy as jnp
from jax import lax
from jax.experimental import pallas as pl
from jax.experimental.pallas import tpu as pltpu
from jax.sharding import PartitionSpec as P

D = 5120
HD = 128
CYCLE = 4


def shifted(value, axis, steps):
    count = lax.axis_size(axis)
    leading, last = (max(0, -steps), min(count, count - steps))
    return lax.ppermute(value, axis, [(source, source + steps) for source in range(leading, last)])


def flipped(value, axis, bit):
    count = lax.axis_size(axis)
    return lax.ppermute(value, axis, [(source, source ^ bit) for source in range(count)])


def ring_kernel(group, tok, scale, q_ref, kv_ref, qdoc_ref, kdoc_ref, o_ref,
                recv, send_sem, recv_sem, m_ref, l_ref, acc_ref, bias_ref):
    c = lax.axis_index("ctx")
    t = lax.axis_index("tp")
    n = lax.axis_size("ctx")
    heads = q_ref.shape[1] // HD
    kv_width = kv_ref.shape[1] // 2
    half = tok // 2

    barrier = pltpu.get_barrier_semaphore()

    @pl.when(c > 0)
    def _():
        pl.semaphore_signal(barrier, inc=1, device_id=(c - 1, t), device_id_type=pl.DeviceIdType.MESH)

    @pl.when(c < n - 1)
    def _():
        pl.semaphore_signal(barrier, inc=1, device_id=(c + 1, t), device_id_type=pl.DeviceIdType.MESH)

    peers = (c > 0).astype(jnp.int32) + (c < n - 1).astype(jnp.int32)
    pl.semaphore_wait(barrier, peers)

    def copy_of(step):
        src = kv_ref if step == 0 else recv.at[step - 1]
        return pltpu.make_async_remote_copy(
            src_ref=src, dst_ref=recv.at[step], send_sem=send_sem.at[step],
            recv_sem=recv_sem.at[step], device_id=(c + 1, t),
            device_id_type=pl.DeviceIdType.MESH)

    def sends_at(step):
        return (c >= step) & (c < n - 1)

    def compute(b, kv, tiles, finish=False):
        for r0, rr, c0, cc in tiles:
            same = qdoc_ref[r0:r0 + rr, :] == kdoc_ref[b:b + 1, c0:c0 + cc]
            if b == 0:
                rows = lax.broadcasted_iota(jnp.int32, (rr, cc), 0) + r0
                cols = lax.broadcasted_iota(jnp.int32, (rr, cc), 1) + c0
                same = same & (cols <= rows)
            bias_ref[r0:r0 + rr, c0:c0 + cc] = jnp.where(same, 0.0, -1e30)

        def pair_of_heads(g, carry):
            kcol = pl.multiple_of(g * HD, HD)
            vcol = pl.multiple_of(kv_width + g * HD, HD)
            for j in range(group):
                h = g * group + j
                qcol = pl.multiple_of(h * HD, HD)
                for r0, rr, c0, cc in tiles:
                    q = q_ref[r0:r0 + rr, pl.ds(qcol, HD)]
                    keys = kv[c0:c0 + cc, pl.ds(kcol, HD)]
                    values = kv[c0:c0 + cc, pl.ds(vcol, HD)]
                    s = lax.dot_general(q, keys, (((1,), (1,)), ((), ())),
                                        preferred_element_type=jnp.float32) * scale
                    s = s + bias_ref[r0:r0 + rr, c0:c0 + cc]
                    top = jnp.max(s, axis=1, keepdims=True)
                    if b == 0:
                        p = jnp.exp(s - top)
                        m_ref[h, r0:r0 + rr, :] = jnp.broadcast_to(top, (rr, HD))
                        l_ref[h, r0:r0 + rr, :] = jnp.broadcast_to(jnp.sum(p, axis=1, keepdims=True), (rr, HD))
                        acc_ref[h, r0:r0 + rr, :] = jnp.dot(
                            p.astype(jnp.bfloat16), values, preferred_element_type=jnp.float32)
                    else:
                        prev = m_ref[h, r0:r0 + rr, :]
                        best = jnp.maximum(prev, top)
                        shrink = jnp.exp(prev - best)
                        p = jnp.exp(s - best[:, :1])
                        m_ref[h, r0:r0 + rr, :] = best
                        l_ref[h, r0:r0 + rr, :] = l_ref[h, r0:r0 + rr, :] * shrink + jnp.sum(p, axis=1, keepdims=True)
                        acc_ref[h, r0:r0 + rr, :] = acc_ref[h, r0:r0 + rr, :] * shrink + jnp.dot(
                            p.astype(jnp.bfloat16), values, preferred_element_type=jnp.float32)
                if finish:
                    o_ref[:, pl.ds(qcol, HD)] = (acc_ref[h] / l_ref[h]).astype(o_ref.dtype)
            return carry

        lax.fori_loop(0, heads // group, pair_of_heads, 0)

    full = [(0, tok, 0, tok)]
    lower = [(0, half, 0, half), (half, half, 0, tok)]
    upper = [(0, half, 0, tok), (half, half, half, half)]
    nback = recv.shape[0]

    @pl.when(c < n - 1)
    def _():
        copy_of(0).start()

    compute(0, kv_ref, lower)
    for s in range(1, nback + 1):
        @pl.when(c >= s)
        def _():
            copy_of(s - 1).wait_recv()

        if s < nback:
            @pl.when(sends_at(s))
            def _():
                copy_of(s).start()

        @pl.when(c >= s)
        def _():
            compute(s, recv.at[s - 1], upper if s == nback else full, finish=s == nback)

    for s in range(nback):
        @pl.when(sends_at(s))
        def _():
            copy_of(s).wait_send()

    def finish(h, carry):
        col = pl.multiple_of(h * HD, HD)
        o_ref[:, pl.ds(col, HD)] = (acc_ref[h] / l_ref[h]).astype(o_ref.dtype)
        return carry

    @pl.when(c < nback)
    def _():
        lax.fori_loop(0, heads, finish, 0)


def ring_attention(queries, kv_local, qdoc, kdoc, kv_heads):
    tok, width = queries.shape
    group = width // HD // kv_heads
    heads = width // HD
    vmem = pltpu.VMEM
    return pl.pallas_call(
        functools.partial(ring_kernel, group, tok, HD ** (-0.5)),
        out_shape=jax.ShapeDtypeStruct((tok, width), queries.dtype),
        in_specs=[pl.BlockSpec(memory_space=vmem)] * 4,
        out_specs=pl.BlockSpec(memory_space=vmem),
        scratch_shapes=[
            vmem((CYCLE, tok, kv_local.shape[1]), kv_local.dtype),
            pltpu.SemaphoreType.DMA((CYCLE,)),
            pltpu.SemaphoreType.DMA((CYCLE,)),
            vmem((heads, tok, HD), jnp.float32),
            vmem((heads, tok, HD), jnp.float32),
            vmem((heads, tok, HD), jnp.float32),
            vmem((tok, tok), jnp.float32),
        ],
        compiler_params=pltpu.CompilerParams(
            collective_id=0, has_side_effects=True, vmem_limit_bytes=48 * 1024 * 1024),
    )(queries, kv_local, qdoc, kdoc)


def body(hidden, queries, lengths, norm_gain, kv_weight, kv_bias):
    tok, width = hidden.shape
    tpi = lax.axis_index("tp")
    own_squares = jnp.sum(jnp.square(hidden.astype(jnp.float32)), axis=1)
    squares_across = flipped(own_squares, "tp", 2)
    squares_beside = flipped(own_squares, "tp", 1)
    squares_diagonal = flipped(squares_across, "tp", 1)
    squares = own_squares + squares_beside + squares_across + squares_diagonal
    scale_rows = lax.rsqrt(squares / D + 1e-06)
    sending, _ = lax.optimization_barrier((hidden, squares_across))
    across = flipped(sending, "tp", 2)
    beside = flipped(hidden, "tp", 1)
    gain_across = flipped(norm_gain, "tp", 2)
    gain_beside = flipped(norm_gain, "tp", 1)
    gain_diagonal = flipped(gain_across, "tp", 1)
    flat_weight = kv_weight.reshape(kv_weight.shape[0], -1)

    def project(part, gain, owner):
        normed = (part.astype(jnp.float32) * scale_rows[:, None] * gain[None, :]).astype(jnp.bfloat16)
        rows = lax.dynamic_slice_in_dim(flat_weight, owner * width, width, 0)
        return jnp.dot(normed, rows, preferred_element_type=jnp.float32)

    summed = project(hidden, norm_gain, tpi) + project(beside, gain_beside, tpi ^ 1)
    across, summed = lax.optimization_barrier((across, summed))
    diagonal = flipped(across, "tp", 1)
    summed = summed + project(across, gain_across, tpi ^ 2)
    summed = summed + project(diagonal, gain_diagonal, tpi ^ 3)
    kv_local = (summed + kv_bias.reshape(-1)[None, :]).astype(jnp.bfloat16)
    kv_heads = kv_weight.shape[2] // HD

    device = lax.axis_index("ctx")
    ends = jnp.cumsum(lengths)
    backs = jnp.arange(CYCLE + 1, dtype=jnp.int32)
    starts = (device - backs) * tok
    positions = starts[:, None] + jnp.arange(tok, dtype=jnp.int32)[None, :]
    found = jnp.sum((positions[:, :, None] >= ends[None, None, :]).astype(jnp.int32), axis=2)
    kdoc = jnp.where((device - backs >= 0)[:, None], found, -1)
    qdoc = found[0]
    kdoc = jnp.concatenate([kdoc, jnp.full((8 - CYCLE - 1, tok), -1, jnp.int32)], axis=0)
    return ring_attention(queries, kv_local, qdoc[:, None], kdoc, kv_heads)


def solution(mesh):
    in_specs = (P("ctx", "tp"), P("ctx", "tp"), P(), P("tp"), P(None, None, "tp"), P(None, "tp"))
    out_specs = P("ctx", "tp")
    return jax.shard_map(body, mesh=mesh, in_specs=in_specs, out_specs=out_specs, check_vma=False)
```

```python
import functools

import jax
import jax.numpy as jnp
from jax import lax
from jax.experimental import pallas as pl
from jax.experimental.pallas import tpu as pltpu
from jax.sharding import PartitionSpec as P

D = 5120
HD = 128
CYCLE = 4


def shifted(value, axis, steps):
    count = lax.axis_size(axis)
    leading, last = (max(0, -steps), min(count, count - steps))
    return lax.ppermute(value, axis, [(source, source + steps) for source in range(leading, last)])


def flipped(value, axis, bit):
    count = lax.axis_size(axis)
    return lax.ppermute(value, axis, [(source, source ^ bit) for source in range(count)])


def ring_kernel(group, tok, scale, q_ref, kv_ref, qdoc_ref, kdoc_ref, o_ref,
                recv, send_sem, recv_sem, m_ref, l_ref, acc_ref, bias_ref):
    c = lax.axis_index("ctx")
    t = lax.axis_index("tp")
    n = lax.axis_size("ctx")
    heads = q_ref.shape[1] // HD
    kv_width = kv_ref.shape[1] // 2
    half = tok // 2

    barrier = pltpu.get_barrier_semaphore()

    @pl.when(c > 0)
    def _():
        pl.semaphore_signal(barrier, inc=1, device_id=(c - 1, t), device_id_type=pl.DeviceIdType.MESH)

    @pl.when(c < n - 1)
    def _():
        pl.semaphore_signal(barrier, inc=1, device_id=(c + 1, t), device_id_type=pl.DeviceIdType.MESH)

    peers = (c > 0).astype(jnp.int32) + (c < n - 1).astype(jnp.int32)
    pl.semaphore_wait(barrier, peers)

    def copy_of(step):
        src = kv_ref if step == 0 else recv.at[step - 1]
        return pltpu.make_async_remote_copy(
            src_ref=src, dst_ref=recv.at[step], send_sem=send_sem.at[step],
            recv_sem=recv_sem.at[step], device_id=(c + 1, t),
            device_id_type=pl.DeviceIdType.MESH)

    def sends_at(step):
        return (c >= step) & (c < n - 1)

    def compute(b, kv, tiles, finish=False):
        for r0, rr, c0, cc in tiles:
            same = qdoc_ref[r0:r0 + rr, :] == kdoc_ref[b:b + 1, c0:c0 + cc]
            if b == 0:
                rows = lax.broadcasted_iota(jnp.int32, (rr, cc), 0) + r0
                cols = lax.broadcasted_iota(jnp.int32, (rr, cc), 1) + c0
                same = same & (cols <= rows)
            bias_ref[r0:r0 + rr, c0:c0 + cc] = jnp.where(same, 0.0, -1e30)

        def pair_of_heads(g, carry):
            kcol = pl.multiple_of(g * HD, HD)
            vcol = pl.multiple_of(kv_width + g * HD, HD)
            for j in range(group):
                h = g * group + j
                qcol = pl.multiple_of(h * HD, HD)
                for r0, rr, c0, cc in tiles:
                    q = q_ref[r0:r0 + rr, pl.ds(qcol, HD)]
                    keys = kv[c0:c0 + cc, pl.ds(kcol, HD)]
                    values = kv[c0:c0 + cc, pl.ds(vcol, HD)]
                    s = lax.dot_general(q, keys, (((1,), (1,)), ((), ())),
                                        preferred_element_type=jnp.float32) * scale
                    s = s + bias_ref[r0:r0 + rr, c0:c0 + cc]
                    top = jnp.max(s, axis=1, keepdims=True)
                    if b == 0:
                        p = jnp.exp(s - top)
                        m_ref[h, r0:r0 + rr, :] = jnp.broadcast_to(top, (rr, HD))
                        l_ref[h, r0:r0 + rr, :] = jnp.broadcast_to(jnp.sum(p, axis=1, keepdims=True), (rr, HD))
                        acc_ref[h, r0:r0 + rr, :] = jnp.dot(
                            p.astype(jnp.bfloat16), values, preferred_element_type=jnp.float32)
                    else:
                        prev = m_ref[h, r0:r0 + rr, :]
                        best = jnp.maximum(prev, top)
                        shrink = jnp.exp(prev - best)
                        p = jnp.exp(s - best[:, :1])
                        m_ref[h, r0:r0 + rr, :] = best
                        l_ref[h, r0:r0 + rr, :] = l_ref[h, r0:r0 + rr, :] * shrink + jnp.sum(p, axis=1, keepdims=True)
                        acc_ref[h, r0:r0 + rr, :] = acc_ref[h, r0:r0 + rr, :] * shrink + jnp.dot(
                            p.astype(jnp.bfloat16), values, preferred_element_type=jnp.float32)
                if finish:
                    o_ref[:, pl.ds(qcol, HD)] = (acc_ref[h] / l_ref[h]).astype(o_ref.dtype)
            return carry

        lax.fori_loop(0, heads // group, pair_of_heads, 0)

    full = [(0, tok, 0, tok)]
    lower = [(0, half, 0, half), (half, half, 0, tok)]
    upper = [(0, half, 0, tok), (half, half, half, half)]
    nback = recv.shape[0]

    @pl.when(c < n - 1)
    def _():
        copy_of(0).start()

    compute(0, kv_ref, lower)
    for s in range(1, nback + 1):
        @pl.when(c >= s)
        def _():
            copy_of(s - 1).wait_recv()

        if s < nback:
            @pl.when(sends_at(s))
            def _():
                copy_of(s).start()

        @pl.when(c >= s)
        def _():
            compute(s, recv.at[s - 1], upper if s == nback else full, finish=s == nback)

    for s in range(nback):
        @pl.when(sends_at(s))
        def _():
            copy_of(s).wait_send()

    def finish(h, carry):
        col = pl.multiple_of(h * HD, HD)
        o_ref[:, pl.ds(col, HD)] = (acc_ref[h] / l_ref[h]).astype(o_ref.dtype)
        return carry

    @pl.when(c < nback)
    def _():
        lax.fori_loop(0, heads, finish, 0)


def ring_attention(queries, kv_local, qdoc, kdoc, kv_heads):
    tok, width = queries.shape
    group = width // HD // kv_heads
    heads = width // HD
    vmem = pltpu.VMEM
    return pl.pallas_call(
        functools.partial(ring_kernel, group, tok, HD ** (-0.5)),
        out_shape=jax.ShapeDtypeStruct((tok, width), queries.dtype),
        in_specs=[pl.BlockSpec(memory_space=vmem)] * 4,
        out_specs=pl.BlockSpec(memory_space=vmem),
        scratch_shapes=[
            vmem((CYCLE, tok, kv_local.shape[1]), kv_local.dtype),
            pltpu.SemaphoreType.DMA((CYCLE,)),
            pltpu.SemaphoreType.DMA((CYCLE,)),
            vmem((heads, tok, HD), jnp.float32),
            vmem((heads, tok, HD), jnp.float32),
            vmem((heads, tok, HD), jnp.float32),
            vmem((tok, tok), jnp.float32),
        ],
        compiler_params=pltpu.CompilerParams(
            collective_id=0, has_side_effects=True, vmem_limit_bytes=48 * 1024 * 1024),
    )(queries, kv_local, qdoc, kdoc)


def body(hidden, queries, lengths, norm_gain, kv_weight, kv_bias):
    tok, width = hidden.shape
    tpi = lax.axis_index("tp")
    own_squares = jnp.sum(jnp.square(hidden.astype(jnp.float32)), axis=1)
    squares_across = flipped(own_squares, "tp", 2)
    squares_beside = flipped(own_squares, "tp", 1)
    squares_diagonal = flipped(squares_across, "tp", 1)
    squares = own_squares + squares_beside + squares_across + squares_diagonal
    scale_rows = lax.rsqrt(squares / D + 1e-06)
    half = tok // 2
    sending, _ = lax.optimization_barrier((hidden[:half], squares_across))
    across_a = flipped(sending, "tp", 2)
    beside = flipped(hidden, "tp", 1)
    gain_across = flipped(norm_gain, "tp", 2)
    gain_beside = flipped(norm_gain, "tp", 1)
    gain_diagonal = flipped(gain_across, "tp", 1)
    flat_weight = kv_weight.reshape(kv_weight.shape[0], -1)

    def project(part, gain, owner, scale):
        normed = (part.astype(jnp.float32) * scale[:, None] * gain[None, :]).astype(jnp.bfloat16)
        rows = lax.dynamic_slice_in_dim(flat_weight, owner * width, width, 0)
        return jnp.dot(normed, rows, preferred_element_type=jnp.float32)

    summed = project(hidden, norm_gain, tpi, scale_rows) + project(beside, gain_beside, tpi ^ 1, scale_rows)
    across_a, summed = lax.optimization_barrier((across_a, summed))
    sending, _ = lax.optimization_barrier((hidden[half:], across_a))
    across_b = flipped(sending, "tp", 2)
    diagonal_a = flipped(across_a, "tp", 1)
    kv_a = (summed[:half] + project(across_a, gain_across, tpi ^ 2, scale_rows[:half])
            + project(diagonal_a, gain_diagonal, tpi ^ 3, scale_rows[:half]))
    across_b, kv_a = lax.optimization_barrier((across_b, kv_a))
    diagonal_b = flipped(across_b, "tp", 1)
    kv_b = (summed[half:] + project(across_b, gain_across, tpi ^ 2, scale_rows[half:])
            + project(diagonal_b, gain_diagonal, tpi ^ 3, scale_rows[half:]))
    summed = jnp.concatenate([kv_a, kv_b], axis=0)
    kv_local = (summed + kv_bias.reshape(-1)[None, :]).astype(jnp.bfloat16)
    kv_heads = kv_weight.shape[2] // HD

    device = lax.axis_index("ctx")
    ends = jnp.cumsum(lengths)
    backs = jnp.arange(CYCLE + 1, dtype=jnp.int32)
    starts = (device - backs) * tok
    positions = starts[:, None] + jnp.arange(tok, dtype=jnp.int32)[None, :]
    found = jnp.sum((positions[:, :, None] >= ends[None, None, :]).astype(jnp.int32), axis=2)
    kdoc = jnp.where((device - backs >= 0)[:, None], found, -1)
    qdoc = found[0]
    kdoc = jnp.concatenate([kdoc, jnp.full((8 - CYCLE - 1, tok), -1, jnp.int32)], axis=0)
    return ring_attention(queries, kv_local, qdoc[:, None], kdoc, kv_heads)


def solution(mesh):
    in_specs = (P("ctx", "tp"), P("ctx", "tp"), P(), P("tp"), P(None, None, "tp"), P(None, "tp"))
    out_specs = P("ctx", "tp")
    return jax.shard_map(body, mesh=mesh, in_specs=in_specs, out_specs=out_specs, check_vma=False)
```

```python
import functools

import jax
import jax.numpy as jnp
from jax import lax
from jax.experimental import pallas as pl
from jax.experimental.pallas import tpu as pltpu
from jax.sharding import PartitionSpec as P

D = 5120
HD = 128
CYCLE = 4


def shifted(value, axis, steps):
    count = lax.axis_size(axis)
    leading, last = (max(0, -steps), min(count, count - steps))
    return lax.ppermute(value, axis, [(source, source + steps) for source in range(leading, last)])


def flipped(value, axis, bit):
    count = lax.axis_size(axis)
    return lax.ppermute(value, axis, [(source, source ^ bit) for source in range(count)])


def ring_kernel(group, tok, scale, q_ref, kv_ref, qdoc_ref, kdoc_ref, o_ref,
                recv, send_sem, recv_sem, m_ref, l_ref, acc_ref, bias_ref):
    c = lax.axis_index("ctx")
    t = lax.axis_index("tp")
    n = lax.axis_size("ctx")
    heads = q_ref.shape[1] // HD
    kv_width = kv_ref.shape[1] // 2
    half = tok // 2

    barrier = pltpu.get_barrier_semaphore()

    @pl.when(c > 0)
    def _():
        pl.semaphore_signal(barrier, inc=1, device_id=(c - 1, t), device_id_type=pl.DeviceIdType.MESH)

    @pl.when(c < n - 1)
    def _():
        pl.semaphore_signal(barrier, inc=1, device_id=(c + 1, t), device_id_type=pl.DeviceIdType.MESH)

    peers = (c > 0).astype(jnp.int32) + (c < n - 1).astype(jnp.int32)
    pl.semaphore_wait(barrier, peers)

    def copy_of(step, part=None):
        src = kv_ref if step == 0 else recv.at[step - 1]
        dst = recv.at[step]
        sem = step
        if part is not None:
            src = src.at[pl.ds(part * half, half)]
            dst = dst.at[pl.ds(part * half, half)]
            sem = step + part
        return pltpu.make_async_remote_copy(
            src_ref=src, dst_ref=dst, send_sem=send_sem.at[sem],
            recv_sem=recv_sem.at[sem], device_id=(c + 1, t),
            device_id_type=pl.DeviceIdType.MESH)

    def sends_at(step):
        return (c >= step) & (c < n - 1)

    def compute(b, kv, tiles, finish=False):
        for r0, rr, c0, cc in tiles:
            same = qdoc_ref[r0:r0 + rr, :] == kdoc_ref[b:b + 1, c0:c0 + cc]
            if b == 0:
                rows = lax.broadcasted_iota(jnp.int32, (rr, cc), 0) + r0
                cols = lax.broadcasted_iota(jnp.int32, (rr, cc), 1) + c0
                same = same & (cols <= rows)
            bias_ref[r0:r0 + rr, c0:c0 + cc] = jnp.where(same, 0.0, -1e30)

        def pair_of_heads(g, carry):
            kcol = pl.multiple_of(g * HD, HD)
            vcol = pl.multiple_of(kv_width + g * HD, HD)
            for j in range(group):
                h = g * group + j
                qcol = pl.multiple_of(h * HD, HD)
                for r0, rr, c0, cc in tiles:
                    q = q_ref[r0:r0 + rr, pl.ds(qcol, HD)]
                    keys = kv[c0:c0 + cc, pl.ds(kcol, HD)]
                    values = kv[c0:c0 + cc, pl.ds(vcol, HD)]
                    s = lax.dot_general(q, keys, (((1,), (1,)), ((), ())),
                                        preferred_element_type=jnp.float32) * scale
                    s = s + bias_ref[r0:r0 + rr, c0:c0 + cc]
                    top = jnp.max(s, axis=1, keepdims=True)
                    if b == 0:
                        p = jnp.exp(s - top)
                        m_ref[h, r0:r0 + rr, :] = jnp.broadcast_to(top, (rr, HD))
                        l_ref[h, r0:r0 + rr, :] = jnp.broadcast_to(jnp.sum(p, axis=1, keepdims=True), (rr, HD))
                        acc_ref[h, r0:r0 + rr, :] = jnp.dot(
                            p.astype(jnp.bfloat16), values, preferred_element_type=jnp.float32)
                    else:
                        prev = m_ref[h, r0:r0 + rr, :]
                        best = jnp.maximum(prev, top)
                        shrink = jnp.exp(prev - best)
                        p = jnp.exp(s - best[:, :1])
                        m_ref[h, r0:r0 + rr, :] = best
                        l_ref[h, r0:r0 + rr, :] = l_ref[h, r0:r0 + rr, :] * shrink + jnp.sum(p, axis=1, keepdims=True)
                        acc_ref[h, r0:r0 + rr, :] = acc_ref[h, r0:r0 + rr, :] * shrink + jnp.dot(
                            p.astype(jnp.bfloat16), values, preferred_element_type=jnp.float32)
                if finish:
                    o_ref[:, pl.ds(qcol, HD)] = (acc_ref[h] / l_ref[h]).astype(o_ref.dtype)
            return carry

        lax.fori_loop(0, heads // group, pair_of_heads, 0)

    full = [(0, tok, 0, tok)]
    lower = [(0, half, 0, half), (half, half, 0, tok)]
    upper = [(0, half, 0, tok), (half, half, half, half)]
    nback = recv.shape[0]

    @pl.when(c < n - 1)
    def _():
        copy_of(0).start()

    def parts_of(step):
        return (0, 1) if step == nback - 1 else (None,)

    compute(0, kv_ref, lower)
    for s in range(1, nback + 1):
        if s < nback:
            @pl.when(c >= s)
            def _():
                copy_of(s - 1).wait_recv()

            @pl.when(sends_at(s))
            def _():
                for part in parts_of(s):
                    copy_of(s, part).start()

            @pl.when(c >= s)
            def _():
                compute(s, recv.at[s - 1], full)
        else:
            @pl.when(c >= s)
            def _():
                copy_of(s - 1, 0).wait_recv()
                compute(s, recv.at[s - 1], [(0, half, 0, half)])
                copy_of(s - 1, 1).wait_recv()
                compute(s, recv.at[s - 1], [(0, half, half, half), (half, half, half, half)], finish=True)

    for s in range(nback):
        @pl.when(sends_at(s))
        def _():
            for part in parts_of(s):
                copy_of(s, part).wait_send()

    def finish(h, carry):
        col = pl.multiple_of(h * HD, HD)
        o_ref[:, pl.ds(col, HD)] = (acc_ref[h] / l_ref[h]).astype(o_ref.dtype)
        return carry

    @pl.when(c < nback)
    def _():
        lax.fori_loop(0, heads, finish, 0)


def ring_attention(queries, kv_local, qdoc, kdoc, kv_heads):
    tok, width = queries.shape
    group = width // HD // kv_heads
    heads = width // HD
    vmem = pltpu.VMEM
    return pl.pallas_call(
        functools.partial(ring_kernel, group, tok, HD ** (-0.5)),
        out_shape=jax.ShapeDtypeStruct((tok, width), queries.dtype),
        in_specs=[pl.BlockSpec(memory_space=vmem)] * 4,
        out_specs=pl.BlockSpec(memory_space=vmem),
        scratch_shapes=[
            vmem((CYCLE, tok, kv_local.shape[1]), kv_local.dtype),
            pltpu.SemaphoreType.DMA((CYCLE + 1,)),
            pltpu.SemaphoreType.DMA((CYCLE + 1,)),
            vmem((heads, tok, HD), jnp.float32),
            vmem((heads, tok, HD), jnp.float32),
            vmem((heads, tok, HD), jnp.float32),
            vmem((tok, tok), jnp.float32),
        ],
        compiler_params=pltpu.CompilerParams(
            collective_id=0, has_side_effects=True, vmem_limit_bytes=48 * 1024 * 1024),
    )(queries, kv_local, qdoc, kdoc)


def body(hidden, queries, lengths, norm_gain, kv_weight, kv_bias):
    tok, width = hidden.shape
    tpi = lax.axis_index("tp")
    own_squares = jnp.sum(jnp.square(hidden.astype(jnp.float32)), axis=1)
    squares_across = flipped(own_squares, "tp", 2)
    squares_beside = flipped(own_squares, "tp", 1)
    squares_diagonal = flipped(squares_across, "tp", 1)
    squares = own_squares + squares_beside + squares_across + squares_diagonal
    scale_rows = lax.rsqrt(squares / D + 1e-06)
    sending, _ = lax.optimization_barrier((hidden, squares_across))
    across = flipped(sending, "tp", 2)
    beside = flipped(hidden, "tp", 1)
    gain_across = flipped(norm_gain, "tp", 2)
    gain_beside = flipped(norm_gain, "tp", 1)
    gain_diagonal = flipped(gain_across, "tp", 1)
    flat_weight = kv_weight.reshape(kv_weight.shape[0], -1)

    def project(part, gain, owner):
        normed = (part.astype(jnp.float32) * scale_rows[:, None] * gain[None, :]).astype(jnp.bfloat16)
        rows = lax.dynamic_slice_in_dim(flat_weight, owner * width, width, 0)
        return jnp.dot(normed, rows, preferred_element_type=jnp.float32)

    summed = project(hidden, norm_gain, tpi) + project(beside, gain_beside, tpi ^ 1)
    across, summed = lax.optimization_barrier((across, summed))
    diagonal = flipped(across, "tp", 1)
    summed = summed + project(across, gain_across, tpi ^ 2)
    summed = summed + project(diagonal, gain_diagonal, tpi ^ 3)
    kv_local = (summed + kv_bias.reshape(-1)[None, :]).astype(jnp.bfloat16)
    kv_heads = kv_weight.shape[2] // HD

    device = lax.axis_index("ctx")
    ends = jnp.cumsum(lengths)
    backs = jnp.arange(CYCLE + 1, dtype=jnp.int32)
    starts = (device - backs) * tok
    positions = starts[:, None] + jnp.arange(tok, dtype=jnp.int32)[None, :]
    found = jnp.sum((positions[:, :, None] >= ends[None, None, :]).astype(jnp.int32), axis=2)
    kdoc = jnp.where((device - backs >= 0)[:, None], found, -1)
    qdoc = found[0]
    kdoc = jnp.concatenate([kdoc, jnp.full((8 - CYCLE - 1, tok), -1, jnp.int32)], axis=0)
    return ring_attention(queries, kv_local, qdoc[:, None], kdoc, kv_heads)


def solution(mesh):
    in_specs = (P("ctx", "tp"), P("ctx", "tp"), P(), P("tp"), P(None, None, "tp"), P(None, "tp"))
    out_specs = P("ctx", "tp")
    return jax.shard_map(body, mesh=mesh, in_specs=in_specs, out_specs=out_specs, check_vma=False)
```

```python
import functools

import jax
import jax.numpy as jnp
from jax import lax
from jax.experimental import pallas as pl
from jax.experimental.pallas import tpu as pltpu
from jax.sharding import PartitionSpec as P

D = 5120
HD = 128
CYCLE = 4


def shifted(value, axis, steps):
    count = lax.axis_size(axis)
    leading, last = (max(0, -steps), min(count, count - steps))
    return lax.ppermute(value, axis, [(source, source + steps) for source in range(leading, last)])


def flipped(value, axis, bit):
    count = lax.axis_size(axis)
    return lax.ppermute(value, axis, [(source, source ^ bit) for source in range(count)])


def ring_kernel(group, tok, scale, q_ref, kv_ref, qdoc_ref, kdoc_ref, o_ref,
                recv, send_sem, recv_sem, m_ref, l_ref, acc_ref, bias_ref):
    c = lax.axis_index("ctx")
    t = lax.axis_index("tp")
    n = lax.axis_size("ctx")
    heads = q_ref.shape[1] // HD
    kv_width = kv_ref.shape[1] // 2
    half = tok // 2

    barrier = pltpu.get_barrier_semaphore()

    @pl.when(c > 0)
    def _():
        pl.semaphore_signal(barrier, inc=1, device_id=(c - 1, t), device_id_type=pl.DeviceIdType.MESH)

    @pl.when(c < n - 1)
    def _():
        pl.semaphore_signal(barrier, inc=1, device_id=(c + 1, t), device_id_type=pl.DeviceIdType.MESH)

    peers = (c > 0).astype(jnp.int32) + (c < n - 1).astype(jnp.int32)
    pl.semaphore_wait(barrier, peers)

    right = jnp.minimum(c + 1, n - 1)

    def copy_of(step):
        src = kv_ref if step == 0 else recv.at[step - 1]
        return pltpu.make_async_remote_copy(
            src_ref=src, dst_ref=recv.at[step], send_sem=send_sem.at[step],
            recv_sem=recv_sem.at[step], device_id=(right, t),
            device_id_type=pl.DeviceIdType.MESH)

    def sends_at(step):
        return (c >= step) & (c < n - 1)

    def compute(b, kv, tiles, finish=False):
        for r0, rr, c0, cc in tiles:
            same = qdoc_ref[r0:r0 + rr, :] == kdoc_ref[b:b + 1, c0:c0 + cc]
            if b == 0:
                rows = lax.broadcasted_iota(jnp.int32, (rr, cc), 0) + r0
                cols = lax.broadcasted_iota(jnp.int32, (rr, cc), 1) + c0
                same = same & (cols <= rows)
            bias_ref[r0:r0 + rr, c0:c0 + cc] = jnp.where(same, 0.0, -1e30)

        def pair_of_heads(g, carry):
            kcol = pl.multiple_of(g * HD, HD)
            vcol = pl.multiple_of(kv_width + g * HD, HD)
            for j in range(group):
                h = g * group + j
                qcol = pl.multiple_of(h * HD, HD)
                for r0, rr, c0, cc in tiles:
                    q = q_ref[r0:r0 + rr, pl.ds(qcol, HD)]
                    keys = kv[c0:c0 + cc, pl.ds(kcol, HD)]
                    values = kv[c0:c0 + cc, pl.ds(vcol, HD)]
                    s = lax.dot_general(q, keys, (((1,), (1,)), ((), ())),
                                        preferred_element_type=jnp.float32) * scale
                    s = s + bias_ref[r0:r0 + rr, c0:c0 + cc]
                    top = jnp.max(s, axis=1, keepdims=True)
                    if b == 0:
                        p = jnp.exp(s - top)
                        m_ref[h, r0:r0 + rr, :] = jnp.broadcast_to(top, (rr, HD))
                        l_ref[h, r0:r0 + rr, :] = jnp.broadcast_to(jnp.sum(p, axis=1, keepdims=True), (rr, HD))
                        acc_ref[h, r0:r0 + rr, :] = jnp.dot(
                            p.astype(jnp.bfloat16), values, preferred_element_type=jnp.float32)
                    else:
                        prev = m_ref[h, r0:r0 + rr, :]
                        best = jnp.maximum(prev, top)
                        shrink = jnp.exp(prev - best)
                        p = jnp.exp(s - best[:, :1])
                        m_ref[h, r0:r0 + rr, :] = best
                        l_ref[h, r0:r0 + rr, :] = l_ref[h, r0:r0 + rr, :] * shrink + jnp.sum(p, axis=1, keepdims=True)
                        acc_ref[h, r0:r0 + rr, :] = acc_ref[h, r0:r0 + rr, :] * shrink + jnp.dot(
                            p.astype(jnp.bfloat16), values, preferred_element_type=jnp.float32)
                if finish:
                    o_ref[:, pl.ds(qcol, HD)] = (acc_ref[h] / l_ref[h]).astype(o_ref.dtype)
            return carry

        lax.fori_loop(0, heads // group, pair_of_heads, 0)

    full = [(0, tok, 0, tok)]
    lower = [(0, half, 0, half), (half, half, 0, tok)]
    upper = [(0, half, 0, tok), (half, half, half, half)]
    nback = recv.shape[0]

    @pl.when(c < n - 1)
    def _():
        copy_of(0).start()

    compute(0, kv_ref, lower)
    for s in range(1, nback + 1):
        @pl.when(c >= s)
        def _():
            copy_of(s - 1).wait_recv()

        if s < nback:
            @pl.when(sends_at(s))
            def _():
                copy_of(s).start()

        @pl.when(c >= s)
        def _():
            compute(s, recv.at[s - 1], upper if s == nback else full, finish=s == nback)

    for s in range(nback):
        @pl.when(sends_at(s))
        def _():
            copy_of(s).wait_send()

    def finish(h, carry):
        col = pl.multiple_of(h * HD, HD)
        o_ref[:, pl.ds(col, HD)] = (acc_ref[h] / l_ref[h]).astype(o_ref.dtype)
        return carry

    @pl.when(c < nback)
    def _():
        lax.fori_loop(0, heads, finish, 0)


def ring_attention(queries, kv_local, qdoc, kdoc, kv_heads):
    tok, width = queries.shape
    group = width // HD // kv_heads
    heads = width // HD
    vmem = pltpu.VMEM
    return pl.pallas_call(
        functools.partial(ring_kernel, group, tok, HD ** (-0.5)),
        out_shape=jax.ShapeDtypeStruct((tok, width), queries.dtype),
        in_specs=[pl.BlockSpec(memory_space=vmem)] * 4,
        out_specs=pl.BlockSpec(memory_space=vmem),
        scratch_shapes=[
            vmem((CYCLE, tok, kv_local.shape[1]), kv_local.dtype),
            pltpu.SemaphoreType.DMA((CYCLE,)),
            pltpu.SemaphoreType.DMA((CYCLE,)),
            vmem((heads, tok, HD), jnp.float32),
            vmem((heads, tok, HD), jnp.float32),
            vmem((heads, tok, HD), jnp.float32),
            vmem((tok, tok), jnp.float32),
        ],
        compiler_params=pltpu.CompilerParams(
            collective_id=0, has_side_effects=True, vmem_limit_bytes=48 * 1024 * 1024),
    )(queries, kv_local, qdoc, kdoc)


def body(hidden, queries, lengths, norm_gain, kv_weight, kv_bias):
    tok, width = hidden.shape
    tpi = lax.axis_index("tp")
    own_squares = jnp.sum(jnp.square(hidden.astype(jnp.float32)), axis=1)
    squares_across = flipped(own_squares, "tp", 2)
    squares_beside = flipped(own_squares, "tp", 1)
    squares_diagonal = flipped(squares_across, "tp", 1)
    squares = own_squares + squares_beside + squares_across + squares_diagonal
    scale_rows = lax.rsqrt(squares / D + 1e-06)
    sending, _ = lax.optimization_barrier((hidden, squares_across))
    across = flipped(sending, "tp", 2)
    beside = flipped(hidden, "tp", 1)
    gain_across = flipped(norm_gain, "tp", 2)
    gain_beside = flipped(norm_gain, "tp", 1)
    gain_diagonal = flipped(gain_across, "tp", 1)
    flat_weight = kv_weight.reshape(kv_weight.shape[0], -1)

    def project(part, gain, owner):
        normed = (part.astype(jnp.float32) * scale_rows[:, None] * gain[None, :]).astype(jnp.bfloat16)
        rows = lax.dynamic_slice_in_dim(flat_weight, owner * width, width, 0)
        return jnp.dot(normed, rows, preferred_element_type=jnp.float32)

    summed = project(hidden, norm_gain, tpi) + project(beside, gain_beside, tpi ^ 1)
    across, summed = lax.optimization_barrier((across, summed))
    diagonal = flipped(across, "tp", 1)
    summed = summed + project(across, gain_across, tpi ^ 2)
    summed = summed + project(diagonal, gain_diagonal, tpi ^ 3)
    kv_local = (summed + kv_bias.reshape(-1)[None, :]).astype(jnp.bfloat16)
    kv_heads = kv_weight.shape[2] // HD

    device = lax.axis_index("ctx")
    ends = jnp.cumsum(lengths)
    backs = jnp.arange(CYCLE + 1, dtype=jnp.int32)
    starts = (device - backs) * tok
    positions = starts[:, None] + jnp.arange(tok, dtype=jnp.int32)[None, :]
    found = jnp.sum((positions[:, :, None] >= ends[None, None, :]).astype(jnp.int32), axis=2)
    kdoc = jnp.where((device - backs >= 0)[:, None], found, -1)
    qdoc = found[0]
    kdoc = jnp.concatenate([kdoc, jnp.full((8 - CYCLE - 1, tok), -1, jnp.int32)], axis=0)
    return ring_attention(queries, kv_local, qdoc[:, None], kdoc, kv_heads)


def solution(mesh):
    in_specs = (P("ctx", "tp"), P("ctx", "tp"), P(), P("tp"), P(None, None, "tp"), P(None, "tp"))
    out_specs = P("ctx", "tp")
    return jax.shard_map(body, mesh=mesh, in_specs=in_specs, out_specs=out_specs, check_vma=False)
```

```python
import functools

import jax
import jax.numpy as jnp
from jax import lax
from jax.experimental import pallas as pl
from jax.experimental.pallas import tpu as pltpu
from jax.sharding import PartitionSpec as P

D = 5120
HD = 128
CYCLE = 4


def shifted(value, axis, steps):
    count = lax.axis_size(axis)
    leading, last = (max(0, -steps), min(count, count - steps))
    return lax.ppermute(value, axis, [(source, source + steps) for source in range(leading, last)])


def flipped(value, axis, bit):
    count = lax.axis_size(axis)
    return lax.ppermute(value, axis, [(source, source ^ bit) for source in range(count)])


def ring_kernel(group, tok, scale, q_ref, kv_ref, qdoc_ref, kdoc_ref, o_ref,
                recv, send_sem, recv_sem, m_ref, l_ref, acc_ref, bias_ref):
    c = lax.axis_index("ctx")
    t = lax.axis_index("tp")
    n = lax.axis_size("ctx")
    heads = q_ref.shape[1] // HD
    kv_width = kv_ref.shape[1] // 2
    half = tok // 2

    barrier = pltpu.get_barrier_semaphore()

    @pl.when(c > 0)
    def _():
        pl.semaphore_signal(barrier, inc=1, device_id=(c - 1, t), device_id_type=pl.DeviceIdType.MESH)

    @pl.when(c < n - 1)
    def _():
        pl.semaphore_signal(barrier, inc=1, device_id=(c + 1, t), device_id_type=pl.DeviceIdType.MESH)

    peers = (c > 0).astype(jnp.int32) + (c < n - 1).astype(jnp.int32)
    pl.semaphore_wait(barrier, peers)

    right = jnp.minimum(c + 1, n - 1)

    def copy_of(step):
        src = kv_ref if step == 0 else recv.at[step - 1]
        return pltpu.make_async_remote_copy(
            src_ref=src, dst_ref=recv.at[step], send_sem=send_sem.at[step],
            recv_sem=recv_sem.at[step], device_id=(right, t),
            device_id_type=pl.DeviceIdType.MESH)

    def sends_at(step):
        return (c >= step) & (c < n - 1)

    def compute(b, kv, tiles, finish=False):
        for r0, rr, c0, cc in tiles:
            same = qdoc_ref[r0:r0 + rr, :] == kdoc_ref[b:b + 1, c0:c0 + cc]
            if b == 0:
                rows = lax.broadcasted_iota(jnp.int32, (rr, cc), 0) + r0
                cols = lax.broadcasted_iota(jnp.int32, (rr, cc), 1) + c0
                same = same & (cols <= rows)
            bias_ref[r0:r0 + rr, c0:c0 + cc] = jnp.where(same, 0.0, -1e30)

        def pair_of_heads(g, carry):
            kcol = pl.multiple_of(g * HD, HD)
            vcol = pl.multiple_of(kv_width + g * HD, HD)
            for j in range(group):
                h = g * group + j
                qcol = pl.multiple_of(h * HD, HD)
                for r0, rr, c0, cc in tiles:
                    q = q_ref[r0:r0 + rr, pl.ds(qcol, HD)]
                    keys = kv[c0:c0 + cc, pl.ds(kcol, HD)]
                    values = kv[c0:c0 + cc, pl.ds(vcol, HD)]
                    s = lax.dot_general(q, keys, (((1,), (1,)), ((), ())),
                                        preferred_element_type=jnp.float32) * scale
                    s = s + bias_ref[r0:r0 + rr, c0:c0 + cc]
                    top = jnp.max(s, axis=1, keepdims=True)
                    if b == 0:
                        p = jnp.exp(s - top)
                        m_ref[h, r0:r0 + rr, :] = jnp.broadcast_to(top, (rr, HD))
                        l_ref[h, r0:r0 + rr, :] = jnp.broadcast_to(jnp.sum(p, axis=1, keepdims=True), (rr, HD))
                        acc_ref[h, r0:r0 + rr, :] = jnp.dot(
                            p.astype(jnp.bfloat16), values, preferred_element_type=jnp.float32)
                    else:
                        prev = m_ref[h, r0:r0 + rr, :]
                        best = jnp.maximum(prev, top)
                        shrink = jnp.exp(prev - best)
                        p = jnp.exp(s - best[:, :1])
                        m_ref[h, r0:r0 + rr, :] = best
                        l_ref[h, r0:r0 + rr, :] = l_ref[h, r0:r0 + rr, :] * shrink + jnp.sum(p, axis=1, keepdims=True)
                        acc_ref[h, r0:r0 + rr, :] = acc_ref[h, r0:r0 + rr, :] * shrink + jnp.dot(
                            p.astype(jnp.bfloat16), values, preferred_element_type=jnp.float32)
                if finish:
                    o_ref[:, pl.ds(qcol, HD)] = (acc_ref[h] / l_ref[h]).astype(o_ref.dtype)
            return carry

        lax.fori_loop(0, heads // group, pair_of_heads, 0)

    full = [(0, tok, 0, tok)]
    lower = [(0, half, 0, half), (half, half, 0, tok)]
    quarter = tok // 4
    upper = [(i * quarter, quarter, i * quarter, tok - i * quarter) for i in range(4)]
    nback = recv.shape[0]

    @pl.when(c < n - 1)
    def _():
        copy_of(0).start()

    compute(0, kv_ref, lower)
    for s in range(1, nback + 1):
        @pl.when(c >= s)
        def _():
            copy_of(s - 1).wait_recv()

        if s < nback:
            @pl.when(sends_at(s))
            def _():
                copy_of(s).start()

        @pl.when(c >= s)
        def _():
            compute(s, recv.at[s - 1], upper if s == nback else full, finish=s == nback)

    for s in range(nback):
        @pl.when(sends_at(s))
        def _():
            copy_of(s).wait_send()

    def finish(h, carry):
        col = pl.multiple_of(h * HD, HD)
        o_ref[:, pl.ds(col, HD)] = (acc_ref[h] / l_ref[h]).astype(o_ref.dtype)
        return carry

    @pl.when(c < nback)
    def _():
        lax.fori_loop(0, heads, finish, 0)


def ring_attention(queries, kv_local, qdoc, kdoc, kv_heads):
    tok, width = queries.shape
    group = width // HD // kv_heads
    heads = width // HD
    vmem = pltpu.VMEM
    return pl.pallas_call(
        functools.partial(ring_kernel, group, tok, HD ** (-0.5)),
        out_shape=jax.ShapeDtypeStruct((tok, width), queries.dtype),
        in_specs=[pl.BlockSpec(memory_space=vmem)] * 4,
        out_specs=pl.BlockSpec(memory_space=vmem),
        scratch_shapes=[
            vmem((CYCLE, tok, kv_local.shape[1]), kv_local.dtype),
            pltpu.SemaphoreType.DMA((CYCLE,)),
            pltpu.SemaphoreType.DMA((CYCLE,)),
            vmem((heads, tok, HD), jnp.float32),
            vmem((heads, tok, HD), jnp.float32),
            vmem((heads, tok, HD), jnp.float32),
            vmem((tok, tok), jnp.float32),
        ],
        compiler_params=pltpu.CompilerParams(
            collective_id=0, has_side_effects=True, vmem_limit_bytes=48 * 1024 * 1024),
    )(queries, kv_local, qdoc, kdoc)


def body(hidden, queries, lengths, norm_gain, kv_weight, kv_bias):
    tok, width = hidden.shape
    tpi = lax.axis_index("tp")
    own_squares = jnp.sum(jnp.square(hidden.astype(jnp.float32)), axis=1)
    squares_across = flipped(own_squares, "tp", 2)
    squares_beside = flipped(own_squares, "tp", 1)
    squares_diagonal = flipped(squares_across, "tp", 1)
    squares = own_squares + squares_beside + squares_across + squares_diagonal
    scale_rows = lax.rsqrt(squares / D + 1e-06)
    sending, _ = lax.optimization_barrier((hidden, squares_across))
    across = flipped(sending, "tp", 2)
    beside = flipped(hidden, "tp", 1)
    gain_across = flipped(norm_gain, "tp", 2)
    gain_beside = flipped(norm_gain, "tp", 1)
    gain_diagonal = flipped(gain_across, "tp", 1)
    flat_weight = kv_weight.reshape(kv_weight.shape[0], -1)

    def project(part, gain, owner):
        normed = (part.astype(jnp.float32) * scale_rows[:, None] * gain[None, :]).astype(jnp.bfloat16)
        rows = lax.dynamic_slice_in_dim(flat_weight, owner * width, width, 0)
        return jnp.dot(normed, rows, preferred_element_type=jnp.float32)

    device = lax.axis_index("ctx")
    ends = jnp.cumsum(lengths)
    backs = jnp.arange(CYCLE + 1, dtype=jnp.int32)
    starts = (device - backs) * tok
    positions = starts[:, None] + jnp.arange(tok, dtype=jnp.int32)[None, :]
    found = jnp.sum((positions[:, :, None] >= ends[None, None, :]).astype(jnp.int32), axis=2)
    kdoc = jnp.where((device - backs >= 0)[:, None], found, -1)
    qdoc = found[0]
    kdoc = jnp.concatenate([kdoc, jnp.full((8 - CYCLE - 1, tok), -1, jnp.int32)], axis=0)

    summed = project(hidden, norm_gain, tpi) + project(beside, gain_beside, tpi ^ 1)
    across, summed, qdoc, kdoc = lax.optimization_barrier((across, summed, qdoc, kdoc))
    diagonal = flipped(across, "tp", 1)
    summed = summed + project(across, gain_across, tpi ^ 2)
    summed = summed + project(diagonal, gain_diagonal, tpi ^ 3)
    kv_local = (summed + kv_bias.reshape(-1)[None, :]).astype(jnp.bfloat16)
    kv_heads = kv_weight.shape[2] // HD

    return ring_attention(queries, kv_local, qdoc[:, None], kdoc, kv_heads)


def solution(mesh):
    in_specs = (P("ctx", "tp"), P("ctx", "tp"), P(), P("tp"), P(None, None, "tp"), P(None, "tp"))
    out_specs = P("ctx", "tp")
    return jax.shard_map(body, mesh=mesh, in_specs=in_specs, out_specs=out_specs, check_vma=False)
```

```python
import functools

import jax
import jax.numpy as jnp
from jax import lax
from jax.experimental import pallas as pl
from jax.experimental.pallas import tpu as pltpu
from jax.sharding import PartitionSpec as P

D = 5120
HD = 128
CYCLE = 4


def shifted(value, axis, steps):
    count = lax.axis_size(axis)
    leading, last = (max(0, -steps), min(count, count - steps))
    return lax.ppermute(value, axis, [(source, source + steps) for source in range(leading, last)])


def flipped(value, axis, bit):
    count = lax.axis_size(axis)
    return lax.ppermute(value, axis, [(source, source ^ bit) for source in range(count)])


def ring_kernel(group, tok, scale, q_ref, kv_ref, qdoc_ref, kdoc_ref, o_ref,
                recv, send_sem, recv_sem, m_ref, l_ref, acc_ref, bias_ref):
    c = lax.axis_index("ctx")
    t = lax.axis_index("tp")
    n = lax.axis_size("ctx")
    heads = q_ref.shape[1] // HD
    kv_width = kv_ref.shape[1] // 2
    half = tok // 2

    barrier = pltpu.get_barrier_semaphore()

    @pl.when(c > 0)
    def _():
        pl.semaphore_signal(barrier, inc=1, device_id=(c - 1, t), device_id_type=pl.DeviceIdType.MESH)

    @pl.when(c < n - 1)
    def _():
        pl.semaphore_signal(barrier, inc=1, device_id=(c + 1, t), device_id_type=pl.DeviceIdType.MESH)

    peers = (c > 0).astype(jnp.int32) + (c < n - 1).astype(jnp.int32)
    pl.semaphore_wait(barrier, peers)

    right = jnp.minimum(c + 1, n - 1)

    def copy_of(step):
        src = kv_ref if step == 0 else recv.at[step - 1]
        return pltpu.make_async_remote_copy(
            src_ref=src, dst_ref=recv.at[step], send_sem=send_sem.at[step],
            recv_sem=recv_sem.at[step], device_id=(right, t),
            device_id_type=pl.DeviceIdType.MESH)

    def sends_at(step):
        return (c >= step) & (c < n - 1)

    def compute(b, kv, tiles, finish=False):
        for r0, rr, c0, cc in tiles:
            same = qdoc_ref[r0:r0 + rr, :] == kdoc_ref[b:b + 1, c0:c0 + cc]
            if b == 0:
                rows = lax.broadcasted_iota(jnp.int32, (rr, cc), 0) + r0
                cols = lax.broadcasted_iota(jnp.int32, (rr, cc), 1) + c0
                same = same & (cols <= rows)
            bias_ref[r0:r0 + rr, c0:c0 + cc] = jnp.where(same, 0.0, -1e30)

        def pair_of_heads(g, carry):
            kcol = pl.multiple_of(g * HD, HD)
            vcol = pl.multiple_of(kv_width + g * HD, HD)
            for j in range(group):
                h = g * group + j
                qcol = pl.multiple_of(h * HD, HD)
                for r0, rr, c0, cc in tiles:
                    q = q_ref[r0:r0 + rr, pl.ds(qcol, HD)]
                    keys = kv[c0:c0 + cc, pl.ds(kcol, HD)]
                    values = kv[c0:c0 + cc, pl.ds(vcol, HD)]
                    s = lax.dot_general(q, keys, (((1,), (1,)), ((), ())),
                                        preferred_element_type=jnp.float32) * scale
                    s = s + bias_ref[r0:r0 + rr, c0:c0 + cc]
                    top = jnp.max(s, axis=1, keepdims=True)
                    if b == 0:
                        p = jnp.exp(s - top)
                        m_ref[h, r0:r0 + rr, :] = jnp.broadcast_to(top, (rr, HD))
                        l_ref[h, r0:r0 + rr, :] = jnp.broadcast_to(jnp.sum(p, axis=1, keepdims=True), (rr, HD))
                        acc_ref[h, r0:r0 + rr, :] = jnp.dot(
                            p.astype(jnp.bfloat16), values, preferred_element_type=jnp.float32)
                    else:
                        prev = m_ref[h, r0:r0 + rr, :]
                        best = jnp.maximum(prev, top)
                        shrink = jnp.exp(prev - best)
                        p = jnp.exp(s - best[:, :1])
                        m_ref[h, r0:r0 + rr, :] = best
                        l_ref[h, r0:r0 + rr, :] = l_ref[h, r0:r0 + rr, :] * shrink + jnp.sum(p, axis=1, keepdims=True)
                        acc_ref[h, r0:r0 + rr, :] = acc_ref[h, r0:r0 + rr, :] * shrink + jnp.dot(
                            p.astype(jnp.bfloat16), values, preferred_element_type=jnp.float32)
                if finish:
                    o_ref[:, pl.ds(qcol, HD)] = (acc_ref[h] / l_ref[h]).astype(o_ref.dtype)
            return carry

        lax.fori_loop(0, heads // group, pair_of_heads, 0)

    full = [(0, tok, 0, tok)]
    lower = [(0, half, 0, half), (half, half, 0, tok)]
    upper = [(0, half, 0, tok), (half, half, half, half)]
    nback = recv.shape[0]

    @pl.when(c < n - 1)
    def _():
        copy_of(0).start()

    compute(0, kv_ref, lower)
    for s in range(1, nback + 1):
        @pl.when(c >= s)
        def _():
            copy_of(s - 1).wait_recv()

        if s < nback:
            @pl.when(sends_at(s))
            def _():
                copy_of(s).start()

        @pl.when(c >= s)
        def _():
            compute(s, recv.at[s - 1], upper if s == nback else full, finish=s == nback)

    for s in range(nback):
        @pl.when(sends_at(s))
        def _():
            copy_of(s).wait_send()

    def finish(h, carry):
        col = pl.multiple_of(h * HD, HD)
        o_ref[:, pl.ds(col, HD)] = (acc_ref[h] / l_ref[h]).astype(o_ref.dtype)
        return carry

    @pl.when(c < nback)
    def _():
        lax.fori_loop(0, heads, finish, 0)


def ring_attention(queries, kv_local, qdoc, kdoc, kv_heads):
    tok, width = queries.shape
    group = width // HD // kv_heads
    heads = width // HD
    vmem = pltpu.VMEM
    return pl.pallas_call(
        functools.partial(ring_kernel, group, tok, HD ** (-0.5)),
        out_shape=jax.ShapeDtypeStruct((tok, width), queries.dtype),
        in_specs=[pl.BlockSpec(memory_space=vmem)] * 4,
        out_specs=pl.BlockSpec(memory_space=vmem),
        scratch_shapes=[
            vmem((CYCLE, tok, kv_local.shape[1]), kv_local.dtype),
            pltpu.SemaphoreType.DMA((CYCLE,)),
            pltpu.SemaphoreType.DMA((CYCLE,)),
            vmem((heads, tok, HD), jnp.float32),
            vmem((heads, tok, HD), jnp.float32),
            vmem((heads, tok, HD), jnp.float32),
            vmem((tok, tok), jnp.float32),
        ],
        compiler_params=pltpu.CompilerParams(
            collective_id=0, has_side_effects=True, vmem_limit_bytes=48 * 1024 * 1024),
    )(queries, kv_local, qdoc, kdoc)


def body(hidden, queries, lengths, norm_gain, kv_weight, kv_bias):
    tok, width = hidden.shape
    tpi = lax.axis_index("tp")
    own_squares = jnp.sum(jnp.square(hidden.astype(jnp.float32)), axis=1)
    squares_across = flipped(own_squares, "tp", 2)
    squares_beside = flipped(own_squares, "tp", 1)
    squares_diagonal = flipped(squares_across, "tp", 1)
    squares = own_squares + squares_beside + squares_across + squares_diagonal
    scale_rows = lax.rsqrt(squares / D + 1e-06)
    sending, _ = lax.optimization_barrier((hidden, squares_across))
    across = flipped(sending, "tp", 2)
    beside = flipped(hidden, "tp", 1)
    gain_across = flipped(norm_gain, "tp", 2)
    gain_beside = flipped(norm_gain, "tp", 1)
    gain_diagonal = flipped(gain_across, "tp", 1)
    flat_weight = kv_weight.reshape(kv_weight.shape[0], -1)

    def project(part, gain, owner):
        normed = (part.astype(jnp.float32) * scale_rows[:, None] * gain[None, :]).astype(jnp.bfloat16)
        rows = lax.dynamic_slice_in_dim(flat_weight, owner * width, width, 0)
        return jnp.dot(normed, rows, preferred_element_type=jnp.float32)

    device = lax.axis_index("ctx")
    ends = jnp.cumsum(lengths)
    backs = jnp.arange(CYCLE + 1, dtype=jnp.int32)
    starts = (device - backs) * tok
    positions = starts[:, None] + jnp.arange(tok, dtype=jnp.int32)[None, :]
    found = jnp.sum((positions[:, :, None] >= ends[None, None, :]).astype(jnp.int32), axis=2)
    kdoc = jnp.where((device - backs >= 0)[:, None], found, -1)
    qdoc = found[0]
    kdoc = jnp.concatenate([kdoc, jnp.full((8 - CYCLE - 1, tok), -1, jnp.int32)], axis=0)

    beside, qdoc, kdoc = lax.optimization_barrier((beside, qdoc, kdoc))
    summed = project(hidden, norm_gain, tpi) + project(beside, gain_beside, tpi ^ 1)
    across, summed = lax.optimization_barrier((across, summed))
    diagonal = flipped(across, "tp", 1)
    summed = summed + project(across, gain_across, tpi ^ 2)
    summed = summed + project(diagonal, gain_diagonal, tpi ^ 3)
    kv_local = (summed + kv_bias.reshape(-1)[None, :]).astype(jnp.bfloat16)
    kv_heads = kv_weight.shape[2] // HD

    return ring_attention(queries, kv_local, qdoc[:, None], kdoc, kv_heads)


def solution(mesh):
    in_specs = (P("ctx", "tp"), P("ctx", "tp"), P(), P("tp"), P(None, None, "tp"), P(None, "tp"))
    out_specs = P("ctx", "tp")
    return jax.shard_map(body, mesh=mesh, in_specs=in_specs, out_specs=out_specs, check_vma=False)
```

```python
import functools

import jax
import jax.numpy as jnp
from jax import lax
from jax.experimental import pallas as pl
from jax.experimental.pallas import tpu as pltpu
from jax.sharding import PartitionSpec as P

D = 5120
HD = 128
CYCLE = 4


def shifted(value, axis, steps):
    count = lax.axis_size(axis)
    leading, last = (max(0, -steps), min(count, count - steps))
    return lax.ppermute(value, axis, [(source, source + steps) for source in range(leading, last)])


def flipped(value, axis, bit):
    count = lax.axis_size(axis)
    return lax.ppermute(value, axis, [(source, source ^ bit) for source in range(count)])


def ring_kernel(group, tok, scale, q_ref, kv_ref, qdoc_ref, kdoc_ref, o_ref,
                recv, send_sem, recv_sem, m_ref, l_ref, acc_ref, bias_ref):
    c = lax.axis_index("ctx")
    t = lax.axis_index("tp")
    n = lax.axis_size("ctx")
    heads = q_ref.shape[1] // HD
    kv_width = kv_ref.shape[1] // 2
    half = tok // 2

    barrier = pltpu.get_barrier_semaphore()

    @pl.when(c > 0)
    def _():
        pl.semaphore_signal(barrier, inc=1, device_id=(c - 1, t), device_id_type=pl.DeviceIdType.MESH)

    @pl.when(c < n - 1)
    def _():
        pl.semaphore_signal(barrier, inc=1, device_id=(c + 1, t), device_id_type=pl.DeviceIdType.MESH)

    peers = (c > 0).astype(jnp.int32) + (c < n - 1).astype(jnp.int32)
    pl.semaphore_wait(barrier, peers)

    def copy_of(step):
        src = kv_ref if step == 0 else recv.at[step - 1]
        return pltpu.make_async_remote_copy(
            src_ref=src, dst_ref=recv.at[step], send_sem=send_sem.at[step],
            recv_sem=recv_sem.at[step], device_id=(c + 1, t),
            device_id_type=pl.DeviceIdType.MESH)

    def sends_at(step):
        return (c >= step) & (c < n - 1)

    m_ref[...] = jnp.full(m_ref.shape, -1e30, jnp.float32)
    l_ref[...] = jnp.zeros(l_ref.shape, jnp.float32)
    acc_ref[...] = jnp.zeros(acc_ref.shape, jnp.float32)

    def compute(b, kv, tiles):
        for r0, rr, c0, cc in tiles:
            same = qdoc_ref[r0:r0 + rr, :] == kdoc_ref[b:b + 1, c0:c0 + cc]
            if b == 0:
                rows = lax.broadcasted_iota(jnp.int32, (rr, cc), 0) + r0
                cols = lax.broadcasted_iota(jnp.int32, (rr, cc), 1) + c0
                same = same & (cols <= rows)
            bias_ref[r0:r0 + rr, c0:c0 + cc] = jnp.where(same, 0.0, -1e30)

        def pair_of_heads(g, carry):
            kcol = pl.multiple_of(g * HD, HD)
            vcol = pl.multiple_of(kv_width + g * HD, HD)
            for j in range(group):
                h = g * group + j
                qcol = pl.multiple_of(h * HD, HD)
                for r0, rr, c0, cc in tiles:
                    q = q_ref[r0:r0 + rr, pl.ds(qcol, HD)]
                    keys = kv[c0:c0 + cc, pl.ds(kcol, HD)]
                    values = kv[c0:c0 + cc, pl.ds(vcol, HD)]
                    s = lax.dot_general(q, keys, (((1,), (1,)), ((), ())),
                                        preferred_element_type=jnp.float32) * scale
                    s = s + bias_ref[r0:r0 + rr, c0:c0 + cc]
                    prev = m_ref[h, r0:r0 + rr, :]
                    top = jnp.max(s, axis=1, keepdims=True)
                    best = jnp.maximum(prev, top)
                    shrink = jnp.exp(prev - best)
                    p = jnp.exp(s - best[:, :1])
                    m_ref[h, r0:r0 + rr, :] = best
                    l_ref[h, r0:r0 + rr, :] = l_ref[h, r0:r0 + rr, :] * shrink + jnp.sum(p, axis=1, keepdims=True)
                    acc_ref[h, r0:r0 + rr, :] = acc_ref[h, r0:r0 + rr, :] * shrink + jnp.dot(
                        p.astype(jnp.bfloat16), values, preferred_element_type=jnp.float32)
            return carry

        lax.fori_loop(0, heads // group, pair_of_heads, 0)

    full = [(0, tok, 0, tok)]
    lower = [(0, half, 0, half), (half, half, 0, tok)]
    upper = [(0, half, 0, tok), (half, half, half, half)]
    nback = recv.shape[0]

    @pl.when(c < n - 1)
    def _():
        copy_of(0).start()

    compute(0, kv_ref, lower)
    for s in range(1, nback + 1):
        @pl.when(c >= s)
        def _():
            copy_of(s - 1).wait_recv()

        if s < nback:
            @pl.when(sends_at(s))
            def _():
                copy_of(s).start()

        @pl.when(c >= s)
        def _():
            compute(s, recv.at[s - 1], upper if s == nback else full)

    for s in range(nback):
        @pl.when(sends_at(s))
        def _():
            copy_of(s).wait_send()

    def finish(h, carry):
        col = pl.multiple_of(h * HD, HD)
        o_ref[:, pl.ds(col, HD)] = (acc_ref[h] / l_ref[h]).astype(o_ref.dtype)
        return carry

    lax.fori_loop(0, heads, finish, 0)


def ring_attention(queries, kv_local, qdoc, kdoc, kv_heads):
    tok, width = queries.shape
    group = width // HD // kv_heads
    heads = width // HD
    vmem = pltpu.VMEM
    return pl.pallas_call(
        functools.partial(ring_kernel, group, tok, HD ** (-0.5)),
        out_shape=jax.ShapeDtypeStruct((tok, width), queries.dtype),
        in_specs=[pl.BlockSpec(memory_space=vmem)] * 4,
        out_specs=pl.BlockSpec(memory_space=vmem),
        scratch_shapes=[
            vmem((CYCLE, tok, kv_local.shape[1]), kv_local.dtype),
            pltpu.SemaphoreType.DMA((CYCLE,)),
            pltpu.SemaphoreType.DMA((CYCLE,)),
            vmem((heads, tok, HD), jnp.float32),
            vmem((heads, tok, HD), jnp.float32),
            vmem((heads, tok, HD), jnp.float32),
            vmem((tok, tok), jnp.float32),
        ],
        compiler_params=pltpu.CompilerParams(
            collective_id=0, has_side_effects=True, vmem_limit_bytes=48 * 1024 * 1024),
    )(queries, kv_local, qdoc, kdoc)


def body(hidden, queries, lengths, norm_gain, kv_weight, kv_bias):
    tok, width = hidden.shape
    tpi = lax.axis_index("tp")
    across = flipped(hidden, "tp", 2)
    own_squares = jnp.sum(jnp.square(hidden.astype(jnp.float32)), axis=1)
    squares_diagonal = flipped(own_squares, "tp", 3)
    squares_beside = flipped(own_squares, "tp", 1)
    squares_across = flipped(squares_diagonal, "tp", 1)
    squares = own_squares + squares_beside + squares_across + squares_diagonal
    scale_rows = lax.rsqrt(squares / D + 1e-06)
    beside = flipped(hidden, "tp", 1)
    gain_diagonal = flipped(norm_gain, "tp", 3)
    gain_beside = flipped(norm_gain, "tp", 1)
    gain_across = flipped(gain_diagonal, "tp", 1)
    flat_weight = kv_weight.reshape(kv_weight.shape[0], -1)

    def project(part, gain, owner):
        normed = (part.astype(jnp.float32) * scale_rows[:, None] * gain[None, :]).astype(jnp.bfloat16)
        rows = lax.dynamic_slice_in_dim(flat_weight, owner * width, width, 0)
        return jnp.dot(normed, rows, preferred_element_type=jnp.float32)

    device = lax.axis_index("ctx")
    ends = jnp.cumsum(lengths)
    backs = jnp.arange(CYCLE + 1, dtype=jnp.int32)
    starts = (device - backs) * tok
    positions = starts[:, None] + jnp.arange(tok, dtype=jnp.int32)[None, :]
    found = jnp.sum((positions[:, :, None] >= ends[None, None, :]).astype(jnp.int32), axis=2)
    kdoc = jnp.where((device - backs >= 0)[:, None], found, -1)
    qdoc = found[0]
    kdoc = jnp.concatenate([kdoc, jnp.full((8 - CYCLE - 1, tok), -1, jnp.int32)], axis=0)

    summed = project(hidden, norm_gain, tpi) + project(beside, gain_beside, tpi ^ 1)
    across, summed, qdoc, kdoc = lax.optimization_barrier((across, summed, qdoc, kdoc))
    diagonal = flipped(across, "tp", 1)
    summed = summed + project(across, gain_across, tpi ^ 2)
    summed = summed + project(diagonal, gain_diagonal, tpi ^ 3)
    kv_local = (summed + kv_bias.reshape(-1)[None, :]).astype(jnp.bfloat16)
    kv_heads = kv_weight.shape[2] // HD

    return ring_attention(queries, kv_local, qdoc[:, None], kdoc, kv_heads)


def solution(mesh):
    in_specs = (P("ctx", "tp"), P("ctx", "tp"), P(), P("tp"), P(None, None, "tp"), P(None, "tp"))
    out_specs = P("ctx", "tp")
    return jax.shard_map(body, mesh=mesh, in_specs=in_specs, out_specs=out_specs, check_vma=False)
```
